256 devices in a mesh: space: 128 (over z, x, y_hi, core), tm: 2 (over y_lo).
Axes of the slice: x: 4, y: 4 (y_hi: 2, y_lo: 2; y = y_hi * 2 + y_lo), z: 8, core: 2. Of those that a mesh axis runs over, the one named last changes fastest.
Arguments:
- features: bfloat16 [128, 2, 2, 512, 128], P('space', 'tm'), may hold values from -6 to 6
- cotangent: bfloat16 [128, 2, 2, 512, 128], P('space', 'tm'), may hold values from -6 to 6
- w_first: bfloat16 [27, 128, 128], replicated, may hold values from -0.109375 to 0.109375
- w_second: bfloat16 [27, 128, 128], replicated, may hold values from -0.109375 to 0.109375
- occupancy: int32 [128, 2, 2, 512], P('space', 'tm'), may hold values from 0 to 1, as said below
- neighbors: int32 [128, 2, 2, 27], P('space', 'tm'), may hold values from -1 to 9, as said below
- send_space: int32 [128, 2, 2, 2], P('space', 'tm'), may hold values from -1 to 1, as said below
- send_time: int32 [128, 2, 4], P('space', 'tm'), may hold values from -1 to 5, as said below
Outputs:
- grad_features: bfloat16 [128, 2, 2, 512, 128], P('space', 'tm')
- grad_first: float32 [27, 128, 128], replicated
- grad_second: float32 [27, 128, 128], replicated
The draws below stay inside these ranges and needn't reach their ends.
Inputs may be any that keep to these rules, and one draw needn't show every extreme that they name: `occupancy`: each device has 1 to 2 active blocks, which come first; on some device all 2 are active. Blocks after the active ones have no occupied voxels. `neighbors`: entries index the extended list of 10 slots; -1 where the neighbouring block is inactive or outside the grid, and in every row of an inactive block. The relation is symmetric: a block's neighbour in one direction has it as neighbour in the opposite direction. `send_space`: positions follow the face's cells; -1 where the cell holds no active block. `send_time`: positions follow the face's cells including one block beyond each slab side, and index the own-plus-space list of 6 slots; -1 where the cell holds no active block or lies outside the grid.
All inputs are finite; a program needn't handle non-finite values.
Results may differ from the reference program's by a relative error of at most 0.0029.
Values may be sent and summed in bfloat16 or wider, within the bound.
No kernel may reach another device: no remote copies, remote signals or barrier semaphores. Data moves between devices by JAX's collectives and lax.ppermute only.
A program may use at most 128 MiB of HBM per device.

```python
import math
import jax
import jax.numpy as jnp
import numpy as np
from jax import lax

CH = 128
EDGE = 8
TAPS = 27
BLK_DEV = 2
VOX = 512
N_SPACE = 128
N_TM = 2


offset_table = np.array([[first, second, third] for first in (-1, 0, 1) for second in (-1, 0, 1) for third in (-1, 0, 1)], dtype=np.int32)


def geometry(key):
    spaces = N_SPACE
    halves = BLK_DEV // 2
    region_cells = 4 * halves
    count_key, pick_key, order_key, dense_key, level_key = jax.random.split(jax.random.fold_in(key, 911), 5)
    counts = jax.random.randint(count_key, (spaces * 2,), halves, BLK_DEV + 1)
    fullest = jax.random.randint(pick_key, (), 0, spaces * 2)
    counts = jnp.where(jnp.arange(spaces * 2) == fullest, BLK_DEV, counts).astype(jnp.int32)
    orders = jax.vmap(lambda subkey: jax.random.permutation(subkey, region_cells))(jax.random.split(order_key, spaces * 2))
    ranked = jnp.argsort(orders, axis=1).astype(jnp.int32)
    slot_of = jnp.where(ranked < counts[:, None], ranked, -1).astype(jnp.int32)
    region = slot_of.reshape(spaces, 2, 2, 2, halves)
    world = region.transpose(1, 2, 0, 3, 4).reshape(4, spaces * 2, halves)
    space_ids = jnp.arange(spaces).reshape(spaces, 1, 1, 1, 1, 1)
    time_ids = jnp.arange(2).reshape(1, 2, 1, 1, 1, 1)
    tblock = jnp.arange(2).reshape(1, 1, 2, 1, 1, 1)
    xblock = jnp.arange(2).reshape(1, 1, 1, 2, 1, 1)
    yblock = jnp.arange(halves).reshape(1, 1, 1, 1, halves, 1)
    step_t = jnp.asarray(offset_table[:, 0]).reshape(1, 1, 1, 1, 1, 27)
    step_x = jnp.asarray(offset_table[:, 1]).reshape(1, 1, 1, 1, 1, 27)
    step_y = jnp.asarray(offset_table[:, 2]).reshape(1, 1, 1, 1, 1, 27)
    near_t = tblock + step_t
    near_x = xblock + step_x
    near_y = yblock + step_y
    global_t = time_ids * 2 + near_t
    global_x = space_ids * 2 + near_x
    valid = (near_y >= 0) & (near_y < halves) & (global_t >= 0) & (global_t < 4) & (global_x >= 0) & (global_x < 2 * spaces)
    found = world[jnp.clip(global_t, 0, 3), jnp.clip(global_x, 0, 2 * spaces - 1), jnp.clip(near_y, 0, halves - 1)]
    live = valid & (found >= 0)
    in_time = (near_t >= 0) & (near_t < 2)
    inside = jnp.where(near_x < 0, BLK_DEV + near_t * halves + near_y, jnp.where(near_x > 1, 2 * BLK_DEV + near_t * halves + near_y, found))
    spot = jnp.where(in_time, inside, 3 * BLK_DEV + (near_x + 1) * halves + near_y)
    rows = jnp.where(live, spot, -1).astype(jnp.int32).reshape(spaces, 2, region_cells, 27)
    select = (slot_of.reshape(spaces, 2, region_cells, 1) == jnp.arange(BLK_DEV).reshape(1, 1, 1, BLK_DEV)).astype(jnp.int32)
    neighbors = (jnp.einsum('stcb,stcd->stbd', select, rows + 1) - 1).astype(jnp.int32)
    down_face = region[:, :, :, 0, :].reshape(spaces, 2, BLK_DEV)
    up_face = region[:, :, :, 1, :].reshape(spaces, 2, BLK_DEV)
    send_space = jnp.stack([down_face, up_face], axis=2).astype(jnp.int32)
    face_t = jnp.where(jnp.arange(2) == 0, 1, 0).reshape(1, 2, 1, 1)
    col_x = (jnp.arange(4) - 1).reshape(1, 1, 4, 1)
    col_y = jnp.arange(halves).reshape(1, 1, 1, halves)
    face_space = jnp.arange(spaces).reshape(spaces, 1, 1, 1)
    face_time = jnp.arange(2).reshape(1, 2, 1, 1)
    face_global_t = face_time * 2 + face_t
    face_global_x = face_space * 2 + col_x
    face_valid = (face_global_x >= 0) & (face_global_x < 2 * spaces)
    face_found = world[face_global_t, jnp.clip(face_global_x, 0, 2 * spaces - 1), col_y]
    face_live = face_valid & (face_found >= 0)
    face_value = jnp.where(col_x < 0, BLK_DEV + face_t * halves + col_y, jnp.where(col_x > 1, 2 * BLK_DEV + face_t * halves + col_y, face_found))
    send_time = jnp.where(face_live, face_value, -1).astype(jnp.int32).reshape(spaces, 2, 2 * BLK_DEV)
    levels = jax.random.randint(level_key, (spaces, 2, BLK_DEV), 35, 95)
    rolls = jax.random.randint(dense_key, (spaces, 2, BLK_DEV, EDGE ** 3), 0, 100)
    active_block = jnp.arange(BLK_DEV).reshape(1, 1, BLK_DEV) < counts.reshape(spaces, 2, 1)
    occupancy = ((rolls < levels[..., None]) & active_block[..., None]).astype(jnp.int32)
    return (neighbors, send_space, send_time, occupancy)


def draw_occupancy(key, part):
    return geometry(key)[3]


def draw_neighbors(key, part):
    return geometry(key)[0]


def draw_send_space(key, part):
    return geometry(key)[1]


def draw_send_time(key, part):
    return geometry(key)[2]


def block_levels(rng, shape, shards, least, largest):
    gain, own = 1.0, jax.random.fold_in(rng, 6)
    for axis_at, shards_of in shards:
        heights = jnp.exp(jax.random.uniform(jax.random.fold_in(own, axis_at), (shards_of,), jnp.float32, least / len(shards), largest / len(shards)))
        gain = gain * jnp.repeat(heights, shape[axis_at] // shards_of).reshape([-1 if axis == axis_at else 1 for axis in range(len(shape))])
    return gain


def noise(key, shape, spread, reach, shards=(), kind=jnp.bfloat16):
    loudness = block_levels(key, shape, shards, -0.22, 0.18) if shards else 1.0
    values = jax.random.normal(key, shape, jnp.float32) * spread * loudness
    return jnp.minimum(jnp.maximum(values, -reach), reach).astype(kind)


def setup_inputs(seed: int = 0) -> dict:
    key_of = jax.random.split(jax.random.key(seed), 9)
    features = noise(key_of[0], (N_SPACE, N_TM, BLK_DEV, VOX, CH), 1.0, 6.0, ((0, 128), (1, 2)))
    cotangent = noise(key_of[1], (N_SPACE, N_TM, BLK_DEV, VOX, CH), 1.0, 6.0, ((0, 128), (1, 2)))
    w_first = noise(key_of[2], (TAPS, CH, CH), (TAPS * CH) ** -0.5, 0.109375)
    w_second = noise(key_of[3], (TAPS, CH, CH), (TAPS * CH) ** -0.5, 0.109375)
    occupancy = draw_occupancy(jax.random.fold_in(key_of[8], 71), 0)
    neighbors = draw_neighbors(jax.random.fold_in(key_of[8], 71), 0)
    send_space = draw_send_space(jax.random.fold_in(key_of[8], 71), 0)
    send_time = draw_send_time(jax.random.fold_in(key_of[8], 71), 0)
    return dict(features=features, cotangent=cotangent, w_first=w_first, w_second=w_second, occupancy=occupancy, neighbors=neighbors, send_space=send_space, send_time=send_time)


offsets = [(first, second, third) for first in (-1, 0, 1) for second in (-1, 0, 1) for third in (-1, 0, 1)]

def rim_spans(component, block_edge):
    if component < 0:
        return (slice(block_edge - 1, block_edge), slice(0, 1))
    if component == 0:
        return (slice(0, block_edge), slice(1, block_edge + 1))
    return (slice(0, 1), slice(block_edge + 1, block_edge + 2))

def assemble(store, table, block_edge):
    total_rows = store.shape[0]
    padded = jnp.concatenate([store, jnp.zeros((1,) + store.shape[1:], store.dtype)], axis=0)
    safe_rows = jnp.where(table < 0, total_rows, table).astype(jnp.int32)
    pieces = {}
    for number, offset in enumerate(offsets):
        source = [rim_spans(component, block_edge)[0] for component in offset]
        pieces[offset] = jnp.take(padded[:, source[0], source[1], source[2]], safe_rows[:, number], axis=0)
    layers = []
    for first in (-1, 0, 1):
        columns = []
        for second in (-1, 0, 1):
            columns.append(jnp.concatenate([pieces[first, second, third] for third in (-1, 0, 1)], axis=3))
        layers.append(jnp.concatenate(columns, axis=2))
    return jnp.concatenate(layers, axis=1)

def window(canvas, offset, block_edge):
    starts = [1 + component for component in offset]
    region = canvas[:, starts[0]:starts[0] + block_edge, starts[1]:starts[1] + block_edge, starts[2]:starts[2] + block_edge]
    return region.reshape(-1, canvas.shape[-1])

def negate(offset):
    return tuple((-component for component in offset))

def dot_transposed(left, weight):
    return lax.dot_general(left, weight, (((1,), (1,)), ((), ())), preferred_element_type=jnp.float32)

def dot_outer(left, right):
    return lax.dot_general(left, right, (((0,), (0,)), ((), ())), preferred_element_type=jnp.float32)

def local_pass(x_tile, g_tile, mask_rows, w_first, w_second, block_edge):
    rows = mask_rows.shape[0]
    channels = w_first.shape[-1]
    pre = jnp.zeros((rows, channels), jnp.float32)
    for number, offset in enumerate(offsets):
        pre = pre + jnp.dot(window(x_tile, offset, block_edge), w_first[number], preferred_element_type=jnp.float32)
    sigmoid_pre = jax.nn.sigmoid(pre)
    hidden = (pre * sigmoid_pre * mask_rows).astype(jnp.bfloat16)
    grad_hidden = jnp.zeros((rows, channels), jnp.float32)
    second_terms = []
    for number, offset in enumerate(offsets):
        back_window = window(g_tile, negate(offset), block_edge)
        grad_hidden = grad_hidden + dot_transposed(back_window, w_second[number])
        second_terms.append(dot_outer(hidden, back_window))
    grad_pre = (grad_hidden * sigmoid_pre * (1.0 + pre * (1.0 - sigmoid_pre)) * mask_rows).astype(jnp.bfloat16)
    first_terms = [dot_outer(window(x_tile, offset, block_edge), grad_pre) for offset in offsets]
    return (grad_pre, jnp.stack(first_terms), jnp.stack(second_terms))

def resolve(neighbors, send_space, send_time):
    spaces, halves_tm, blocks = (neighbors.shape[0], neighbors.shape[1], neighbors.shape[2])
    rim_slots = send_space.shape[3]
    space_ids = jnp.arange(spaces).astype(jnp.int32)[:, None, None]
    time_ids = jnp.arange(halves_tm).astype(jnp.int32)[None, :, None]

    def owner(space_index, time_index, slot_value):
        return jnp.where(slot_value >= 0, (space_index * halves_tm + time_index) * blocks + slot_value, -1).astype(jnp.int32)
    own_slots = jnp.broadcast_to(jnp.arange(blocks).astype(jnp.int32)[None, None, :], (spaces, halves_tm, blocks))
    own_ids = owner(space_ids, time_ids, own_slots)
    empty_row = jnp.full((1, halves_tm, rim_slots), -1, jnp.int32)
    lower_src = jnp.concatenate([empty_row, send_space[:-1, :, 1, :]], axis=0)
    upper_src = jnp.concatenate([send_space[1:, :, 0, :], empty_row], axis=0)
    below_ids = owner(space_ids - 1, time_ids, lower_src)
    above_ids = owner(space_ids + 1, time_ids, upper_src)
    base_ids = jnp.concatenate([own_ids, below_ids, above_ids], axis=2)
    peer_base = base_ids[:, ::-1]
    peer_send = send_time[:, ::-1]
    taken = jnp.take_along_axis(peer_base, jnp.maximum(peer_send, 0), axis=2)
    across_ids = jnp.where(peer_send >= 0, taken, -1).astype(jnp.int32)
    extended = jnp.concatenate([base_ids, across_ids], axis=2)
    wide = jnp.broadcast_to(extended[:, :, None, :], (spaces, halves_tm, blocks, extended.shape[2]))
    looked = jnp.take_along_axis(wide, jnp.maximum(neighbors, 0), axis=3)
    return jnp.where(neighbors >= 0, looked, -1).astype(jnp.int32)

def reference(features, cotangent, w_first, w_second, occupancy, neighbors, send_space, send_time):
    spaces, halves_tm, blocks, voxels, channels = features.shape
    block_edge = EDGE
    units = spaces * halves_tm
    mask_cells = occupancy.reshape(units, blocks, voxels, 1).astype(jnp.bfloat16)
    mask_rows = occupancy.reshape(units, blocks * voxels, 1).astype(jnp.float32)
    masked_x = features.reshape(units, blocks, voxels, channels) * mask_cells
    masked_g = cotangent.reshape(units, blocks, voxels, channels) * mask_cells
    store_x = masked_x.reshape(units * blocks, block_edge, block_edge, block_edge, channels)
    store_g = masked_g.reshape(units * blocks, block_edge, block_edge, block_edge, channels)
    table = resolve(neighbors, send_space, send_time).reshape(units, blocks, TAPS)

    def forward_unit(carry, inputs):
        unit_table, unit_mask = inputs
        x_tile = assemble(store_x, unit_table, block_edge)
        g_tile = assemble(store_g, unit_table, block_edge)
        grad_pre, first_part, second_part = local_pass(x_tile, g_tile, unit_mask, w_first, w_second, block_edge)
        return ((carry[0] + first_part, carry[1] + second_part), grad_pre)
    zeros_weight = jnp.zeros((TAPS, channels, channels), jnp.float32)
    sums, grad_pre_all = lax.scan(forward_unit, (zeros_weight, zeros_weight), (table, mask_rows))
    store_da = grad_pre_all.reshape(units * blocks, block_edge, block_edge, block_edge, channels)
    cot_rows = cotangent.reshape(units, blocks * voxels, channels)

    def input_unit(inputs):
        unit_table, unit_mask, unit_cot = inputs
        da_tile = assemble(store_da, unit_table, block_edge)
        total = jnp.zeros((blocks * voxels, channels), jnp.float32)
        for number, offset in enumerate(offsets):
            total = total + dot_transposed(window(da_tile, negate(offset), block_edge), w_first[number])
        return (unit_cot.astype(jnp.float32) + total * unit_mask).astype(jnp.bfloat16)
    grad_rows = lax.map(input_unit, (table, mask_rows, cot_rows))
    scale = 1.0 / math.sqrt(units * blocks * voxels)
    return (grad_rows.reshape(features.shape), sums[0] * scale, sums[1] * scale)
```

```python
import functools
import math

import jax
import jax.numpy as jnp
from jax import lax
from jax.experimental import pallas as pl
from jax.experimental.pallas import tpu as pltpu
from jax.sharding import Mesh
from jax.sharding import PartitionSpec as P

SPLIT = {"z": 8, "x": 4, "yh": 2, "c": 2}
SPACE = ("z", "x", "yh", "c")
TIME = "yl"
PLANE = ("x", "yh", "yl")

E = 8
CH = 128
FACE = E * E
VOX = E * FACE
BLK = 2
ROWS = BLK * VOX
BF = jnp.bfloat16
F32 = jnp.float32

WINDOWS = [(dt, dx) for dt in (-1, 0, 1) for dx in (-1, 0, 1)]

VM = pl.BlockSpec(memory_space=pltpu.VMEM)
SM = pl.BlockSpec(memory_space=pltpu.SMEM)
PARAMS = pltpu.CompilerParams(vmem_limit_bytes=56 * 1024 * 1024)


def pick(index, options, shape, dtype):
    value = jnp.zeros(shape, dtype)
    for number, option in options:
        value = jnp.where(index == number, option, value)
    return value


def store_faces(values, sends, half, refs):
    prev_ref, next_ref, time_ref, prev_diag, next_diag = refs
    for i, blocks in enumerate(values):
        planes = [block.reshape(E, FACE, CH) for block in blocks]
        lows = [plane[:, :E].reshape(FACE, CH) for plane in planes]
        highs = [plane[:, FACE - E :].reshape(FACE, CH) for plane in planes]
        times = [jnp.where(half == 0, plane[E - 1], plane[0]) for plane in planes]
        for slot in range(BLK):
            time_ref[i, slot] = times[slot].astype(time_ref.dtype)
            low, high = sends[0, slot], sends[1, slot]
            prev_ref[i, slot] = pick(low, list(enumerate(lows)), (FACE, CH), F32).astype(BF)
            next_ref[i, slot] = pick(high, list(enumerate(highs)), (FACE, CH), F32).astype(BF)
            prev_diag[i, slot] = pick(
                low, [(b, t[:E]) for b, t in enumerate(times)], (E, CH), F32
            ).astype(BF)
            next_diag[i, slot] = pick(
                high, [(b, t[FACE - E :]) for b, t in enumerate(times)], (E, CH), F32
            ).astype(BF)


def face_shapes(n):
    return [
        jax.ShapeDtypeStruct((n, BLK, rows, CH), BF) for rows in (FACE, FACE, FACE, E, E)
    ]


def pack_kernel(sends, half, f_ref, g_ref, occ_ref, xg_ref, mask_ref, *faces):
    values = [[], []]
    for b in range(BLK):
        row = occ_ref[b : b + 1, :].astype(F32)
        mask = jnp.broadcast_to(row, (CH, VOX)).T
        mask_ref[b] = mask
        for i, ref in enumerate((f_ref, g_ref)):
            masked = ref[b].astype(F32) * mask
            xg_ref[i, b] = masked.astype(BF)
            values[i].append(masked)
    store_faces(values, sends, half[0], faces)


def build(tile, n, own, table, peer, halos):
    below, above, across, below_diag, above_diag = halos
    end = FACE + E
    for b in range(BLK):
        for i in range(n):
            tile[i, b, 1 : E + 1, E:end] = own[i, b].astype(F32).reshape(E, FACE, CH)
    for b in range(BLK):
        for dt in (-1, 0, 1):
            for dx in (-1, 0, 1):
                if dt == 0 and dx == 0:
                    continue
                slot = table[b, (dt + 1) * 9 + (dx + 1) * 3 + 1]
                side, side_diag = (below, below_diag) if dx < 0 else (above, above_diag)
                first = BLK if dx < 0 else 2 * BLK
                far = peer[jnp.clip(slot - 3 * BLK, 0, 2 * BLK - 1)]
                far = jnp.where(slot >= 3 * BLK, far, -1)
                for i in range(n):
                    if dt == 0:
                        rows = slice(FACE - E, FACE) if dx < 0 else slice(0, E)
                        where = slice(0, E) if dx < 0 else slice(end, end + E)
                        value = jnp.zeros((E, E, CH), F32)
                        for j in range(BLK):
                            face = own[i, j].astype(F32).reshape(E, FACE, CH)[:, rows]
                            value = jnp.where(slot == j, face, value)
                            halo = side[i, j].astype(F32).reshape(E, E, CH)
                            value = jnp.where(slot == first + j, halo, value)
                        tile[i, b, 1 : E + 1, where] = value
                        continue
                    plane = slice(VOX - FACE, VOX) if dt < 0 else slice(0, FACE)
                    to = 0 if dt < 0 else E + 1
                    if dx == 0:
                        value = jnp.zeros((FACE, CH), F32)
                        for j in range(BLK):
                            value = jnp.where(slot == j, own[i, j, plane].astype(F32), value)
                            value = jnp.where(far == j, across[i, j].astype(F32), value)
                        tile[i, b, to, E:end] = value
                        continue
                    rows = slice(FACE - E, FACE) if dx < 0 else slice(0, E)
                    where = slice(0, E) if dx < 0 else slice(end, end + E)
                    value = jnp.zeros((E, CH), F32)
                    for j in range(BLK):
                        edge = own[i, j, plane].astype(F32)[rows]
                        value = jnp.where(slot == j, edge, value)
                        edge = side[i, j].astype(F32)
                        edge = edge[FACE - E :] if dt < 0 else edge[:E]
                        value = jnp.where(slot == first + j, edge, value)
                        edge = across[i, j].astype(F32)[rows]
                        value = jnp.where(far == j, edge, value)
                        value = jnp.where(far == first + j, side_diag[i, j].astype(F32), value)
                    tile[i, b, to, where] = value


def columns(tile, i, sign, cols):
    for w, (dt, dx) in enumerate(WINDOWS):
        t, x = 1 + sign * dt, E * (1 + sign * dx)
        for b in range(BLK):
            window = tile[i, b, t : t + E, x : x + FACE].reshape(VOX, CH)
            cols[b * VOX : (b + 1) * VOX, w * CH : (w + 1) * CH] = window.astype(BF)


def shift(value, step):
    y = lax.broadcasted_iota(jnp.int32, value.shape, 0) % E
    moved = pltpu.roll(value, (-step) % value.shape[0], 0)
    return jnp.where(y == (E - 1 if step > 0 else 0), 0.0, moved)


def lanes(value, dy):
    return value[:, (dy + 1) * CH : (dy + 2) * CH]


def gather_y(parts, sign):
    return lanes(parts, 0) + shift(lanes(parts, 1), sign) + shift(lanes(parts, -1), -sign)


def transposed(cols, w_ref, wide):
    for k in range(27):
        w, d = divmod(k, 3)
        wide[d * CH : (d + 1) * CH, w * CH : (w + 1) * CH] = w_ref[k]
    parts = lax.dot_general(
        cols[...], wide[...], (((1,), (1,)), ((), ())), preferred_element_type=F32
    )
    return gather_y(parts, -1)


def outer(left, right):
    return lax.dot_general(left, right, (((0,), (0,)), ((), ())), preferred_element_type=F32)


def local_kernel(
    table, peer, sends, half, core, xg, mask_ref, w1, w2, h0, h1, h2, h3, h4,
    gp_ref, keep_ref, send_ref, f0, f1, f2, f3, f4, tile, xcol, gcol, wide, tall,
):
    build(tile, 2, xg, table, peer, (h0, h1, h2, h3, h4))
    columns(tile, 0, 1, xcol)
    columns(tile, 1, -1, gcol)
    mask = mask_ref[...].reshape(ROWS, CH)
    for k in range(27):
        w, d = divmod(k, 3)
        tall[w * CH : (w + 1) * CH, d * CH : (d + 1) * CH] = w1[k]
    parts = jnp.dot(xcol[...], tall[...], preferred_element_type=F32)
    pre = gather_y(parts, 1)
    sig = jax.nn.sigmoid(pre)
    hidden = (pre * sig * mask).astype(BF).astype(F32)
    shifted = jnp.concatenate([shift(hidden, -1), hidden, shift(hidden, 1)], axis=1).astype(BF)
    second = outer(shifted, gcol[...])
    grad_hidden = transposed(gcol, w2, wide)
    grad_pre = (grad_hidden * sig * (1.0 + pre * (1.0 - sig)) * mask).astype(BF)
    gp_ref[...] = grad_pre.reshape(1, BLK, VOX, CH)
    grad_pre = grad_pre.astype(F32)
    blocks = [[grad_pre[b * VOX : (b + 1) * VOX] for b in range(BLK)]]
    store_faces(blocks, sends, half[0], (f0, f1, f2, f3, f4))
    shifted = jnp.concatenate(
        [shift(grad_pre, 1), grad_pre, shift(grad_pre, -1)], axis=1
    ).astype(BF)
    first = outer(xcol[...], shifted)
    mine = core[0] == 0
    for k in range(27):
        w, d = divmod(k, 3)
        a = second[d * CH : (d + 1) * CH, w * CH : (w + 1) * CH]
        b = first[w * CH : (w + 1) * CH, d * CH : (d + 1) * CH]
        keep_ref[k] = jnp.where(mine, a, b)
        send_ref[k] = jnp.where(mine, b, a).astype(BF)


def input_kernel(
    table, peer, gp, mask_ref, cot, w1, h0, h1, h2, h3, h4, out, tile, dcol, wide
):
    build(tile, 1, gp, table, peer, (h0, h1, h2, h3, h4))
    columns(tile, 0, -1, dcol)
    total = transposed(dcol, w1, wide) * mask_ref[...].reshape(ROWS, CH)
    total = cot[...].astype(F32).reshape(ROWS, CH) + total
    out[...] = total.astype(BF).reshape(BLK, VOX, CH)


def pack(f, g, occ, sends, half):
    return pl.pallas_call(
        pack_kernel,
        out_shape=[
            jax.ShapeDtypeStruct((2, BLK, VOX, CH), BF),
            jax.ShapeDtypeStruct((BLK, VOX, CH), F32),
            *face_shapes(2),
        ],
        in_specs=[SM, SM, VM, VM, VM],
        out_specs=[VM] * 7,
        compiler_params=PARAMS,
        name="pack",
    )(sends, half, f, g, occ)


def local_pass(table, peer, sends, half, core, xg, mask, w1, w2, halos):
    return pl.pallas_call(
        local_kernel,
        out_shape=[
            jax.ShapeDtypeStruct((1, BLK, VOX, CH), BF),
            jax.ShapeDtypeStruct((27, CH, CH), F32),
            jax.ShapeDtypeStruct((27, CH, CH), BF),
            *face_shapes(1),
        ],
        in_specs=[SM] * 5 + [VM] * 9,
        out_specs=[VM] * 8,
        scratch_shapes=[
            pltpu.VMEM((2, BLK, E + 2, (E + 2) * E, CH), F32),
            pltpu.VMEM((ROWS, 9 * CH), BF),
            pltpu.VMEM((ROWS, 9 * CH), BF),
            pltpu.VMEM((3 * CH, 9 * CH), BF),
            pltpu.VMEM((9 * CH, 3 * CH), BF),
        ],
        compiler_params=PARAMS,
        name="local_pass",
    )(table, peer, sends, half, core, xg, mask, w1, w2, *halos)


def input_grad(table, peer, gp, mask, cot, w1, halos):
    return pl.pallas_call(
        input_kernel,
        out_shape=jax.ShapeDtypeStruct((BLK, VOX, CH), BF),
        in_specs=[SM] * 2 + [VM] * 9,
        out_specs=VM,
        scratch_shapes=[
            pltpu.VMEM((1, BLK, E + 2, (E + 2) * E, CH), F32),
            pltpu.VMEM((ROWS, 9 * CH), BF),
            pltpu.VMEM((3 * CH, 9 * CH), BF),
        ],
        compiler_params=PARAMS,
        name="input_grad",
    )(table, peer, gp, mask, cot, w1, *halos)


def swap(value, axis):
    return lax.ppermute(value, axis, [(0, 1), (1, 0)])


def exchange(faces):
    to_prev, to_next, to_time, to_prev_diag, to_next_diag = faces
    size = math.prod(lax.axis_size(axis) for axis in SPACE)
    up = [(i, i + 1) for i in range(size - 1)]
    down = [(i + 1, i) for i in range(size - 1)]
    cross = lambda pairs: [(2 * i + t, 2 * j + 1 - t) for i, j in pairs for t in (0, 1)]
    both = (*SPACE, TIME)
    return (
        lax.ppermute(to_next, SPACE, up),
        lax.ppermute(to_prev, SPACE, down),
        swap(to_time, TIME),
        lax.ppermute(to_next_diag, both, cross(up)),
        lax.ppermute(to_prev_diag, both, cross(down)),
    )


def spread(value, axes):
    size = math.prod(lax.axis_size(axis) for axis in axes)
    copies = jnp.broadcast_to(value[None], (size, *value.shape))
    return lax.all_to_all(copies, axes, 0, 0)


def reduce_all(keep, send, scale):
    total = keep + swap(send, "c").astype(F32)
    plane = math.prod(lax.axis_size(axis) for axis in PLANE)
    rows = 27 * CH // plane
    parts = lax.all_to_all(total.astype(BF).reshape(plane, rows, CH), PLANE, 0, 0)
    total = jnp.sum(parts.astype(F32), axis=0)
    depth = lax.axis_size("z")
    parts = lax.all_to_all(total.reshape(depth, rows // depth, CH), "z", 0, 0)
    total = (jnp.sum(parts, axis=0) * scale).astype(BF)
    total = spread(total, ("z",)).reshape(rows, CH)
    mine = spread(total, PLANE).reshape(27, CH, CH)
    other = swap(mine, "c")
    even = lax.axis_index("c") == 0
    second = jnp.where(even, mine, other).astype(F32)
    first = jnp.where(even, other, mine).astype(F32)
    return first, second


def body(features, cotangent, w_first, w_second, occupancy, neighbors, send_space, send_time):
    f, g = (a.reshape(BLK, VOX, CH) for a in (features, cotangent))
    half = lax.axis_index(TIME).astype(jnp.int32).reshape(1)
    core = lax.axis_index("c").astype(jnp.int32).reshape(1)
    sends = send_space.reshape(2, BLK)
    table = neighbors.reshape(BLK, 27)
    peer = swap(send_time.reshape(2 * BLK), TIME)
    xg, mask, *faces = pack(f, g, occupancy.reshape(BLK, VOX), sends, half)
    halos = exchange(faces)
    gp, keep, send, *faces = local_pass(
        table, peer, sends, half, core, xg, mask, w_first, w_second, halos
    )
    halos = exchange(faces)
    out = input_grad(table, peer, gp, mask, g, w_first, halos)
    devices = math.prod(lax.axis_size(axis) for axis in (*SPACE, TIME))
    first, second = reduce_all(keep, send, 1.0 / math.sqrt(devices * ROWS))
    return out.reshape(features.shape), first, second


def solution(mesh):
    fine = Mesh(
        mesh.devices.reshape(*SPLIT.values(), mesh.shape["tm"]), (*SPACE, TIME)
    )
    split = lambda rank: P(SPACE, TIME, *[None] * (rank - 2))
    return jax.shard_map(
        body,
        mesh=fine,
        in_specs=(
            split(5), split(5), P(), P(), split(4), split(4), split(4), split(3),
        ),
        out_specs=(split(5), P(), P()),
        check_vma=False,
    )
```

```python
import functools
import math

import jax
import jax.numpy as jnp
from jax import lax
from jax.experimental import pallas as pl
from jax.experimental.pallas import tpu as pltpu
from jax.sharding import Mesh
from jax.sharding import PartitionSpec as P

SPLIT = {"z": 8, "x": 4, "yh": 2, "c": 2}
SPACE = ("z", "x", "yh", "c")
TIME = "yl"
PLANE = ("x", "yh", "yl")

E = 8
CH = 128
FACE = E * E
VOX = E * FACE
BLK = 2
ROWS = BLK * VOX
RIM = 4 * FACE + 4 * E
BF = jnp.bfloat16
F32 = jnp.float32

WINDOWS = [(dt, dx) for dt in (-1, 0, 1) for dx in (-1, 0, 1)]

VM = pl.BlockSpec(memory_space=pltpu.VMEM)
SM = pl.BlockSpec(memory_space=pltpu.SMEM)
PARAMS = pltpu.CompilerParams(vmem_limit_bytes=56 * 1024 * 1024)


def stack_rows(parts):
    return jnp.concatenate([part.reshape(-1, CH) for part in parts], axis=0)


def pack_kernel(sends, when, half, core, f_ref, g_ref, occ_ref, xg_ref, mask_ref, *messages):
    even_ref, odd_ref, time_ref, even_diag, odd_diag = messages
    even = core[0] == 0
    sides, times, corners = [], [], []
    for b in range(BLK):
        row = occ_ref[b : b + 1, :].astype(F32)
        mask = jnp.broadcast_to(row, (CH, VOX)).T
        mask_ref[b] = mask
        values = []
        for i, ref in enumerate((f_ref, g_ref)):
            masked = ref[b].astype(F32) * mask
            xg_ref[i, b] = masked.astype(BF)
            values.append(masked.reshape(E, FACE, CH))
        mask = mask.reshape(E, FACE, CH)
        low = stack_rows([v[:, : 2 * E] for v in values] + [mask[:, :E]])
        high = stack_rows([v[:, FACE - 2 * E :] for v in values] + [mask[:, FACE - E :]])
        sides.append((low, high))
        first = half[0] == 0
        edge = [jnp.where(first, v[E - 2 :], v[:2]) for v in values]
        edge.append(jnp.where(first, mask[E - 1 :], mask[:1]))
        times.append(stack_rows(edge))
        pad = jnp.zeros((E, CH), F32)
        low = stack_rows([v[:, : 2 * E] for v in edge[:2]] + [edge[2][:, :E], pad])
        high = stack_rows(
            [v[:, FACE - 2 * E :] for v in edge[:2]] + [edge[2][:, FACE - E :], pad]
        )
        corners.append((low, high))
    rows = lax.broadcasted_iota(jnp.int32, (2 * E, CH), 0)
    note = jnp.zeros((2 * E, CH), F32)
    for p in range(2 * BLK):
        note = jnp.where(rows == p, when[p].astype(F32), note)
    for side_ref, diag_ref, up in ((even_ref, even_diag, even), (odd_ref, odd_diag, ~even)):
        for slot in range(BLK):
            index = jnp.where(up, sends[1, slot], sends[0, slot])
            for ref, options in ((side_ref, sides), (diag_ref, corners)):
                value = jnp.zeros(options[0][0].shape, F32)
                for b, (low, high) in enumerate(options):
                    value = jnp.where(index == b, jnp.where(up, high, low), value)
                ref[slot] = value.astype(BF)
    for b in range(BLK):
        time_ref[b] = jnp.concatenate([times[b], note], axis=0).astype(BF)


def select(flag, value, other):
    if flag.ndim == 0:
        return jnp.where(flag, value, other)
    tiles = lambda v: v.reshape(-1, E, CH)
    chosen = jnp.where(jnp.broadcast_to(flag, tiles(value).shape), tiles(value), tiles(other))
    return chosen.reshape(value.shape)


def build(targets, owns, table, even, halos):
    even_side, odd_side, across, even_diag, odd_diag = (
        [ref[j].astype(F32) for j in range(BLK)] for ref in halos
    )
    either = lambda a, b: [jnp.where(even, p, q) for p, q in zip(a, b)]
    below, below_diag = either(odd_side, even_side), either(odd_diag, even_diag)
    above, above_diag = either(even_side, odd_side), either(even_diag, odd_diag)
    notes = [
        jnp.broadcast_to(across[0][5 * FACE + p : 5 * FACE + p + 1], (E, CH))
        for p in range(2 * BLK)
    ]
    for (tile, w, _, _), own in zip(targets, owns):
        for b in range(BLK):
            tile[b, w : w + E, w * E : w * E + FACE] = own[b]
    for b in range(BLK):
        for dt, dx in WINDOWS:
            if dt == 0 and dx == 0:
                continue
            slot = table[b, (dt + 1) * 9 + (dx + 1) * 3 + 1]
            side, diag = (below, below_diag) if dx < 0 else (above, above_diag)
            first = BLK if dx < 0 else 2 * BLK
            far = jnp.full((E, CH), -1.0, F32)
            for p, note in enumerate(notes):
                far = jnp.where(slot == 3 * BLK + p, note, far)
            for (tile, w, row, corner), own in zip(targets, owns):
                ts = {-1: slice(E - w, E), 0: slice(0, E), 1: slice(0, w)}[dt]
                xs = {-1: slice(FACE - w * E, FACE), 0: slice(0, FACE), 1: slice(0, w * E)}[dx]
                to_t = {-1: slice(0, w), 0: slice(w, w + E), 1: slice(w + E, 2 * w + E)}[dt]
                end = w * E + FACE
                to_x = {-1: slice(0, w * E), 0: slice(w * E, end), 1: slice(end, end + w * E)}[dx]
                value = jnp.zeros(own[0][ts, xs].shape, F32)
                for j in range(BLK):
                    value = select(slot == j, own[j][ts, xs], value)
                    if dx != 0:
                        face = side[j][row : row + FACE * w].reshape(E, w * E, CH)
                        value = select(slot == first + j, face[ts], value)
                    if dt != 0:
                        face = across[j][row : row + FACE * w].reshape(w, FACE, CH)
                        value = select(far == j, face[:, xs], value)
                    if dt != 0 and dx != 0:
                        face = diag[j][corner : corner + E * w * w].reshape(w, w * E, CH)
                        value = select(far == first + j, face, value)
                tile[b, to_t, to_x] = value


def pieces(tile, b, w, dt, dx):
    cut = lambda t, nt, x, nx: tile[
        b, w + t + dt : w + t + dt + nt, E * (w + x + dx) : E * (w + x + dx + nx)
    ].reshape(nt * nx * E, CH)
    rim = [(-1, 1, -1, E + 2), (E, 1, -1, E + 2), (0, E, -1, 1), (0, E, E, 1)]
    return cut(0, E, 0, E), lambda: [cut(*part) for part in rim]


def columns(tile, w, sign, cols, rim):
    for k, (dt, dx) in enumerate(WINDOWS):
        lane = slice(k * CH, (k + 1) * CH)
        for b in range(BLK):
            core, ring = pieces(tile, b, w, sign * dt, sign * dx)
            cols[b * VOX : (b + 1) * VOX, lane] = core.astype(BF)
            if rim:
                at = ROWS + b * RIM
                cols[at : at + RIM, lane] = jnp.concatenate(ring(), axis=0).astype(BF)


def shift(value, step):
    y = lax.broadcasted_iota(jnp.int32, value.shape, 0) % E
    moved = pltpu.roll(value, (-step) % value.shape[0], 0)
    return jnp.where(y == (E - 1 if step > 0 else 0), 0.0, moved)


def lanes(value, dy):
    return value[:, (dy + 1) * CH : (dy + 2) * CH]


def gather_y(parts, sign):
    return lanes(parts, 0) + shift(lanes(parts, 1), sign) + shift(lanes(parts, -1), -sign)


def transposed(cols, w_ref, wide):
    for k in range(27):
        w, d = divmod(k, 3)
        wide[d * CH : (d + 1) * CH, w * CH : (w + 1) * CH] = w_ref[k]
    parts = lax.dot_general(
        cols[...], wide[...], (((1,), (1,)), ((), ())), preferred_element_type=F32
    )
    return gather_y(parts, -1)


def outer(left, right):
    return lax.dot_general(left, right, (((0,), (0,)), ((), ())), preferred_element_type=F32)


def local_kernel(
    table, core, xg, mask_ref, w1, w2, h0, h1, h2, h3, h4,
    gp_ref, keep_ref, send_ref, xtile, gtile, mtile, xcol, gcol, wide, tall,
):
    owns = [[xg[i, b].astype(F32).reshape(E, FACE, CH) for b in range(BLK)] for i in range(2)]
    owns.append([mask_ref[b].reshape(E, FACE, CH) for b in range(BLK)])
    targets = [
        (xtile, 2, 0, 0),
        (gtile, 2, 2 * FACE, 4 * E),
        (mtile, 1, 4 * FACE, 8 * E),
    ]
    even = core[0] == 0
    build(targets, owns, table, even, (h0, h1, h2, h3, h4))
    columns(xtile, 2, 1, xcol, True)
    columns(gtile, 2, -1, gcol, True)
    parts = [pieces(mtile, b, 1, 0, 0) for b in range(BLK)]
    mask = jnp.concatenate([p[0] for p in parts] + parts[0][1]() + parts[1][1](), axis=0)
    for k in range(27):
        w, d = divmod(k, 3)
        tall[w * CH : (w + 1) * CH, d * CH : (d + 1) * CH] = w1[k]
    parts = jnp.dot(xcol[...], tall[...], preferred_element_type=F32)
    pre = gather_y(parts, 1)
    sig = jax.nn.sigmoid(pre)
    hidden = (pre[:ROWS] * sig[:ROWS] * mask[:ROWS]).astype(BF).astype(F32)
    shifted = jnp.concatenate([shift(hidden, -1), hidden, shift(hidden, 1)], axis=1).astype(BF)
    second = outer(shifted, gcol[:ROWS])
    grad_hidden = transposed(gcol, w2, wide)
    grad_pre = (grad_hidden * sig * (1.0 + pre * (1.0 - sig)) * mask).astype(BF).astype(F32)
    for b in range(BLK):
        at = ROWS + b * RIM
        side = (E + 2) * E
        gp_ref[b, 1 : E + 1, E : E + FACE] = grad_pre[b * VOX : (b + 1) * VOX].reshape(E, FACE, CH)
        gp_ref[b, 0] = grad_pre[at : at + side]
        gp_ref[b, E + 1] = grad_pre[at + side : at + 2 * side]
        at += 2 * side
        gp_ref[b, 1 : E + 1, 0:E] = grad_pre[at : at + FACE].reshape(E, E, CH)
        gp_ref[b, 1 : E + 1, E + FACE :] = grad_pre[at + FACE : at + 2 * FACE].reshape(E, E, CH)
    grad_pre = grad_pre[:ROWS]
    shifted = jnp.concatenate(
        [shift(grad_pre, 1), grad_pre, shift(grad_pre, -1)], axis=1
    ).astype(BF)
    first = outer(xcol[:ROWS], shifted)
    for k in range(27):
        w, d = divmod(k, 3)
        a = second[d * CH : (d + 1) * CH, w * CH : (w + 1) * CH]
        b = first[w * CH : (w + 1) * CH, d * CH : (d + 1) * CH]
        keep_ref[k] = jnp.where(even, a, b)
        send_ref[k] = jnp.where(even, b, a).astype(BF)


def input_kernel(gp, mask_ref, cot, w1, out, dcol, wide):
    columns(gp, 1, -1, dcol, False)
    total = transposed(dcol, w1, wide) * mask_ref[...].reshape(ROWS, CH)
    total = cot[...].astype(F32).reshape(ROWS, CH) + total
    out[...] = total.astype(BF).reshape(BLK, VOX, CH)


def pack(f, g, occ, sends, when, half, core):
    shapes = [5 * FACE, 5 * FACE, 5 * FACE + 2 * E, 10 * E, 10 * E]
    return pl.pallas_call(
        pack_kernel,
        out_shape=[
            jax.ShapeDtypeStruct((2, BLK, VOX, CH), BF),
            jax.ShapeDtypeStruct((BLK, VOX, CH), F32),
            *[jax.ShapeDtypeStruct((BLK, rows, CH), BF) for rows in shapes],
        ],
        in_specs=[SM] * 4 + [VM] * 3,
        out_specs=[VM] * 7,
        compiler_params=PARAMS,
        name="pack",
    )(sends, when, half, core, f, g, occ)


def local_pass(table, core, xg, mask, w1, w2, halos):
    return pl.pallas_call(
        local_kernel,
        out_shape=[
            jax.ShapeDtypeStruct((BLK, E + 2, (E + 2) * E, CH), F32),
            jax.ShapeDtypeStruct((27, CH, CH), F32),
            jax.ShapeDtypeStruct((27, CH, CH), BF),
        ],
        in_specs=[SM] * 2 + [VM] * 9,
        out_specs=[VM] * 3,
        scratch_shapes=[
            pltpu.VMEM((BLK, E + 4, (E + 4) * E, CH), F32),
            pltpu.VMEM((BLK, E + 4, (E + 4) * E, CH), F32),
            pltpu.VMEM((BLK, E + 2, (E + 2) * E, CH), F32),
            pltpu.VMEM((ROWS + BLK * RIM, 9 * CH), BF),
            pltpu.VMEM((ROWS + BLK * RIM, 9 * CH), BF),
            pltpu.VMEM((3 * CH, 9 * CH), BF),
            pltpu.VMEM((9 * CH, 3 * CH), BF),
        ],
        compiler_params=PARAMS,
        name="local_pass",
    )(table, core, xg, mask, w1, w2, *halos)


def input_grad(gp, mask, cot, w1):
    return pl.pallas_call(
        input_kernel,
        out_shape=jax.ShapeDtypeStruct((BLK, VOX, CH), BF),
        in_specs=[VM] * 4,
        out_specs=VM,
        scratch_shapes=[
            pltpu.VMEM((ROWS, 9 * CH), BF),
            pltpu.VMEM((3 * CH, 9 * CH), BF),
        ],
        compiler_params=PARAMS,
        name="input_grad",
    )(gp, mask, cot, w1)


def swap(value, axis):
    return lax.ppermute(value, axis, [(0, 1), (1, 0)])


def exchange(messages):
    even_side, odd_side, time, even_diag, odd_diag = messages
    size = math.prod(lax.axis_size(axis) for axis in SPACE)
    both = lambda start: [
        pair for i in range(start, size - 1, 2) for pair in ((i, i + 1), (i + 1, i))
    ]
    cross = lambda pairs: [(2 * i + t, 2 * j + 1 - t) for i, j in pairs for t in (0, 1)]
    return (
        lax.ppermute(even_side, SPACE, both(0)),
        lax.ppermute(odd_side, SPACE, both(1)),
        swap(time, TIME),
        lax.ppermute(even_diag, (*SPACE, TIME), cross(both(0))),
        lax.ppermute(odd_diag, (*SPACE, TIME), cross(both(1))),
    )


def spread(value, axes):
    size = math.prod(lax.axis_size(axis) for axis in axes)
    copies = jnp.broadcast_to(value[None], (size, *value.shape))
    return lax.all_to_all(copies, axes, 0, 0)


def reduce_all(keep, send, scale):
    total = keep + swap(send, "c").astype(F32)
    plane = math.prod(lax.axis_size(axis) for axis in PLANE)
    rows = 27 * CH // plane
    parts = lax.all_to_all(total.astype(BF).reshape(plane, rows, CH), PLANE, 0, 0)
    total = jnp.sum(parts.astype(F32), axis=0)
    depth = lax.axis_size("z")
    parts = lax.all_to_all(total.reshape(depth, rows // depth, CH), "z", 0, 0)
    total = (jnp.sum(parts, axis=0) * scale).astype(BF)
    total = spread(total, ("z",)).reshape(rows, CH)
    mine = spread(total, PLANE).reshape(27, CH, CH)
    other = swap(mine, "c")
    even = lax.axis_index("c") == 0
    second = jnp.where(even, mine, other).astype(F32)
    first = jnp.where(even, other, mine).astype(F32)
    return first, second


def body(features, cotangent, w_first, w_second, occupancy, neighbors, send_space, send_time):
    f, g = (a.reshape(BLK, VOX, CH) for a in (features, cotangent))
    half = lax.axis_index(TIME).astype(jnp.int32).reshape(1)
    core = lax.axis_index("c").astype(jnp.int32).reshape(1)
    sends = send_space.reshape(2, BLK)
    table = neighbors.reshape(BLK, 27)
    when = send_time.reshape(2 * BLK)
    xg, mask, *messages = pack(f, g, occupancy.reshape(BLK, VOX), sends, when, half, core)
    halos = exchange(messages)
    gp, keep, send = local_pass(table, core, xg, mask, w_first, w_second, halos)
    out = input_grad(gp, mask, g, w_first)
    devices = math.prod(lax.axis_size(axis) for axis in (*SPACE, TIME))
    first, second = reduce_all(keep, send, 1.0 / math.sqrt(devices * ROWS))
    return out.reshape(features.shape), first, second


def solution(mesh):
    fine = Mesh(
        mesh.devices.reshape(*SPLIT.values(), mesh.shape["tm"]), (*SPACE, TIME)
    )
    split = lambda rank: P(SPACE, TIME, *[None] * (rank - 2))
    return jax.shard_map(
        body,
        mesh=fine,
        in_specs=(
            split(5), split(5), P(), P(), split(4), split(4), split(4), split(3),
        ),
        out_specs=(split(5), P(), P()),
        check_vma=False,
    )
```

```python
import functools
import math

import jax
import jax.numpy as jnp
from jax import lax
from jax.experimental import pallas as pl
from jax.experimental.pallas import tpu as pltpu
from jax.sharding import Mesh
from jax.sharding import PartitionSpec as P

SPLIT = {"z": 8, "x": 4, "yh": 2, "c": 2}
SPACE = ("z", "x", "yh", "c")
TIME = "yl"
PLANE = ("x", "yh", "yl")

E = 8
CH = 128
FACE = E * E
VOX = E * FACE
BLK = 2
ROWS = BLK * VOX
RIM = 4 * FACE + 4 * E
BF = jnp.bfloat16
F32 = jnp.float32

WINDOWS = [(dt, dx) for dt in (-1, 0, 1) for dx in (-1, 0, 1)]

VM = pl.BlockSpec(memory_space=pltpu.VMEM)
SM = pl.BlockSpec(memory_space=pltpu.SMEM)
PARAMS = pltpu.CompilerParams(vmem_limit_bytes=32 * 1024 * 1024)


def stack_rows(parts):
    return jnp.concatenate([part.reshape(-1, CH) for part in parts], axis=0)


def pack_kernel(sends, when, half, core, f_ref, g_ref, occ_ref, xg_ref, mask_ref, *messages):
    even_ref, odd_ref, time_ref, even_diag, odd_diag = messages
    even = core[0] == 0
    sides, times, corners = [], [], []
    for b in range(BLK):
        row = occ_ref[b : b + 1, :].astype(F32)
        mask = jnp.broadcast_to(row, (CH, VOX)).T
        mask_ref[b] = mask
        values = []
        for i, ref in enumerate((f_ref, g_ref)):
            masked = ref[b].astype(F32) * mask
            xg_ref[i, b] = masked.astype(BF)
            values.append(masked.reshape(E, FACE, CH))
        mask = mask.reshape(E, FACE, CH)
        low = stack_rows([v[:, : 2 * E] for v in values] + [mask[:, :E]])
        high = stack_rows([v[:, FACE - 2 * E :] for v in values] + [mask[:, FACE - E :]])
        sides.append((low, high))
        first = half[0] == 0
        edge = [jnp.where(first, v[E - 2 :], v[:2]) for v in values]
        edge.append(jnp.where(first, mask[E - 1 :], mask[:1]))
        times.append(stack_rows(edge))
        pad = jnp.zeros((E, CH), F32)
        low = stack_rows([v[:, : 2 * E] for v in edge[:2]] + [edge[2][:, :E], pad])
        high = stack_rows(
            [v[:, FACE - 2 * E :] for v in edge[:2]] + [edge[2][:, FACE - E :], pad]
        )
        corners.append((low, high))
    rows = lax.broadcasted_iota(jnp.int32, (2 * E, CH), 0)
    note = jnp.zeros((2 * E, CH), F32)
    for p in range(2 * BLK):
        note = jnp.where(rows == p, when[p].astype(F32), note)
    for side_ref, diag_ref, up in ((even_ref, even_diag, even), (odd_ref, odd_diag, ~even)):
        for slot in range(BLK):
            index = jnp.where(up, sends[1, slot], sends[0, slot])
            for ref, options in ((side_ref, sides), (diag_ref, corners)):
                value = jnp.zeros(options[0][0].shape, F32)
                for b, (low, high) in enumerate(options):
                    value = jnp.where(index == b, jnp.where(up, high, low), value)
                ref[slot] = value.astype(BF)
    for b in range(BLK):
        time_ref[b] = jnp.concatenate([times[b], note], axis=0).astype(BF)


def select(flag, value, other):
    if flag.ndim == 0:
        return jnp.where(flag, value, other)
    tiles = lambda v: v.reshape(-1, E, CH)
    chosen = jnp.where(jnp.broadcast_to(flag, tiles(value).shape), tiles(value), tiles(other))
    return chosen.reshape(value.shape)


def build(targets, owns, table, even, halos):
    even_side, odd_side, across, even_diag, odd_diag = (
        [ref[j].astype(F32) for j in range(BLK)] for ref in halos
    )
    either = lambda a, b: [jnp.where(even, p, q) for p, q in zip(a, b)]
    below, below_diag = either(odd_side, even_side), either(odd_diag, even_diag)
    above, above_diag = either(even_side, odd_side), either(even_diag, odd_diag)
    notes = [
        jnp.broadcast_to(across[0][5 * FACE + p : 5 * FACE + p + 1], (E, CH))
        for p in range(2 * BLK)
    ]
    for (tile, w, _, _), own in zip(targets, owns):
        for b in range(BLK):
            tile[b, w : w + E, w * E : w * E + FACE] = own[b]
    for b in range(BLK):
        for dt, dx in WINDOWS:
            if dt == 0 and dx == 0:
                continue
            slot = table[b, (dt + 1) * 9 + (dx + 1) * 3 + 1]
            side, diag = (below, below_diag) if dx < 0 else (above, above_diag)
            first = BLK if dx < 0 else 2 * BLK
            far = jnp.full((E, CH), -1.0, F32)
            for p, note in enumerate(notes):
                far = jnp.where(slot == 3 * BLK + p, note, far)
            for (tile, w, row, corner), own in zip(targets, owns):
                ts = {-1: slice(E - w, E), 0: slice(0, E), 1: slice(0, w)}[dt]
                xs = {-1: slice(FACE - w * E, FACE), 0: slice(0, FACE), 1: slice(0, w * E)}[dx]
                to_t = {-1: slice(0, w), 0: slice(w, w + E), 1: slice(w + E, 2 * w + E)}[dt]
                end = w * E + FACE
                to_x = {-1: slice(0, w * E), 0: slice(w * E, end), 1: slice(end, end + w * E)}[dx]
                value = jnp.zeros(own[0][ts, xs].shape, F32)
                for j in range(BLK):
                    value = select(slot == j, own[j][ts, xs], value)
                    if dx != 0:
                        face = side[j][row : row + FACE * w].reshape(E, w * E, CH)
                        value = select(slot == first + j, face[ts], value)
                    if dt != 0:
                        face = across[j][row : row + FACE * w].reshape(w, FACE, CH)
                        value = select(far == j, face[:, xs], value)
                    if dt != 0 and dx != 0:
                        face = diag[j][corner : corner + E * w * w].reshape(w, w * E, CH)
                        value = select(far == first + j, face, value)
                tile[b, to_t, to_x] = value


def pieces(tile, b, w, dt, dx):
    cut = lambda t, nt, x, nx: tile[
        b, w + t + dt : w + t + dt + nt, E * (w + x + dx) : E * (w + x + dx + nx)
    ].reshape(nt * nx * E, CH)
    rim = [(-1, 1, -1, E + 2), (E, 1, -1, E + 2), (0, E, -1, 1), (0, E, E, 1)]
    return cut(0, E, 0, E), lambda: [cut(*part) for part in rim]


def columns(tile, w, sign, cols, blocks, rim):
    for k, (dt, dx) in enumerate(WINDOWS):
        lane = slice(k * CH, (k + 1) * CH)
        for i, b in enumerate(blocks):
            core, ring = pieces(tile, b, w, sign * dt, sign * dx)
            cols[i * VOX : (i + 1) * VOX, lane] = core.astype(BF)
            if rim:
                at = ROWS + i * RIM
                cols[at : at + RIM, lane] = jnp.concatenate(ring(), axis=0).astype(BF)


def shift(value, step):
    y = lax.broadcasted_iota(jnp.int32, value.shape, 0) % E
    moved = pltpu.roll(value, (-step) % value.shape[0], 0)
    return jnp.where(y == (E - 1 if step > 0 else 0), 0.0, moved)


def lanes(value, dy):
    return value[:, (dy + 1) * CH : (dy + 2) * CH]


def gather_y(parts, sign):
    return lanes(parts, 0) + shift(lanes(parts, 1), sign) + shift(lanes(parts, -1), -sign)


def transposed(cols, w_ref, wide):
    for k in range(27):
        w, d = divmod(k, 3)
        wide[d * CH : (d + 1) * CH, w * CH : (w + 1) * CH] = w_ref[k]
    parts = lax.dot_general(
        cols[...], wide[...], (((1,), (1,)), ((), ())), preferred_element_type=F32
    )
    return gather_y(parts, -1)


def outer(left, right):
    return lax.dot_general(left, right, (((0,), (0,)), ((), ())), preferred_element_type=F32)


def local_kernel(
    table, core, xg, mask_ref, w1, w2, h0, h1, h2, h3, h4,
    gp_ref, keep_ref, send_ref, xtile, gtile, mtile, xcol, gcol, wide, tall,
):
    owns = [[xg[i, b].astype(F32).reshape(E, FACE, CH) for b in range(BLK)] for i in range(2)]
    owns.append([mask_ref[b].reshape(E, FACE, CH) for b in range(BLK)])
    targets = [
        (xtile, 2, 0, 0),
        (gtile, 2, 2 * FACE, 4 * E),
        (mtile, 1, 4 * FACE, 8 * E),
    ]
    even = core[0] == 0
    build(targets, owns, table, even, (h0, h1, h2, h3, h4))
    columns(xtile, 2, 1, xcol, range(BLK), True)
    columns(gtile, 2, -1, gcol, range(BLK), True)
    parts = [pieces(mtile, b, 1, 0, 0) for b in range(BLK)]
    mask = jnp.concatenate([p[0] for p in parts] + parts[0][1]() + parts[1][1](), axis=0)
    for k in range(27):
        w, d = divmod(k, 3)
        tall[w * CH : (w + 1) * CH, d * CH : (d + 1) * CH] = w1[k]
    parts = jnp.dot(xcol[...], tall[...], preferred_element_type=F32)
    pre = gather_y(parts, 1)
    sig = jax.nn.sigmoid(pre)
    hidden = (pre[:ROWS] * sig[:ROWS] * mask[:ROWS]).astype(BF).astype(F32)
    shifted = jnp.concatenate([shift(hidden, -1), hidden, shift(hidden, 1)], axis=1).astype(BF)
    second = outer(shifted, gcol[:ROWS])
    grad_hidden = transposed(gcol, w2, wide)
    grad_pre = (grad_hidden * sig * (1.0 + pre * (1.0 - sig)) * mask).astype(BF).astype(F32)
    for b in range(BLK):
        at = ROWS + b * RIM
        side = (E + 2) * E
        gp_ref[b, 1 : E + 1, E : E + FACE] = grad_pre[b * VOX : (b + 1) * VOX].reshape(E, FACE, CH)
        gp_ref[b, 0] = grad_pre[at : at + side]
        gp_ref[b, E + 1] = grad_pre[at + side : at + 2 * side]
        at += 2 * side
        gp_ref[b, 1 : E + 1, 0:E] = grad_pre[at : at + FACE].reshape(E, E, CH)
        gp_ref[b, 1 : E + 1, E + FACE :] = grad_pre[at + FACE : at + 2 * FACE].reshape(E, E, CH)
    grad_pre = grad_pre[:ROWS]
    shifted = jnp.concatenate(
        [shift(grad_pre, 1), grad_pre, shift(grad_pre, -1)], axis=1
    ).astype(BF)
    first = outer(xcol[:ROWS], shifted)
    for k in range(27):
        w, d = divmod(k, 3)
        a = second[d * CH : (d + 1) * CH, w * CH : (w + 1) * CH]
        b = first[w * CH : (w + 1) * CH, d * CH : (d + 1) * CH]
        keep_ref[k] = jnp.where(even, a, b)
        send_ref[k] = jnp.where(even, b, a).astype(BF)


def input_kernel(block, gp, mask_ref, cot, w1, *refs):
    *before, out, dcol, wide = refs
    columns(gp, 1, -1, dcol, [block], False)
    total = transposed(dcol, w1, wide) * mask_ref[block]
    total = (cot[block].astype(F32) + total).astype(BF)
    if before:
        out[:block] = before[0][...]
        out[block] = total
    else:
        out[0] = total


def pack(f, g, occ, sends, when, half, core):
    shapes = [5 * FACE, 5 * FACE, 5 * FACE + 2 * E, 10 * E, 10 * E]
    return pl.pallas_call(
        pack_kernel,
        out_shape=[
            jax.ShapeDtypeStruct((2, BLK, VOX, CH), BF),
            jax.ShapeDtypeStruct((BLK, VOX, CH), F32),
            *[jax.ShapeDtypeStruct((BLK, rows, CH), BF) for rows in shapes],
        ],
        in_specs=[SM] * 4 + [VM] * 3,
        out_specs=[VM] * 7,
        compiler_params=PARAMS,
        name="pack",
    )(sends, when, half, core, f, g, occ)


def local_pass(table, core, xg, mask, w1, w2, halos):
    return pl.pallas_call(
        local_kernel,
        out_shape=[
            jax.ShapeDtypeStruct((BLK, E + 2, (E + 2) * E, CH), F32),
            jax.ShapeDtypeStruct((27, CH, CH), F32),
            jax.ShapeDtypeStruct((27, CH, CH), BF),
        ],
        in_specs=[SM] * 2 + [VM] * 9,
        out_specs=[VM] * 3,
        scratch_shapes=[
            pltpu.VMEM((BLK, E + 4, (E + 4) * E, CH), F32),
            pltpu.VMEM((BLK, E + 4, (E + 4) * E, CH), F32),
            pltpu.VMEM((BLK, E + 2, (E + 2) * E, CH), F32),
            pltpu.VMEM((ROWS + BLK * RIM, 9 * CH), BF),
            pltpu.VMEM((ROWS + BLK * RIM, 9 * CH), BF),
            pltpu.VMEM((3 * CH, 9 * CH), BF),
            pltpu.VMEM((9 * CH, 3 * CH), BF),
        ],
        compiler_params=PARAMS,
        name="local_pass",
    )(table, core, xg, mask, w1, w2, *halos)


def input_grad(block, gp, mask, cot, w1, *before):
    return pl.pallas_call(
        functools.partial(input_kernel, block),
        out_shape=jax.ShapeDtypeStruct((BLK if before else 1, VOX, CH), BF),
        in_specs=[VM] * (4 + len(before)),
        out_specs=VM,
        scratch_shapes=[
            pltpu.VMEM((VOX, 9 * CH), BF),
            pltpu.VMEM((3 * CH, 9 * CH), BF),
        ],
        compiler_params=PARAMS,
        name="input_grad%d" % block,
    )(gp, mask, cot, w1, *before)


def swap(value, axis):
    return lax.ppermute(value, axis, [(0, 1), (1, 0)])


def exchange(messages):
    even_side, odd_side, time, even_diag, odd_diag = messages
    size = math.prod(lax.axis_size(axis) for axis in SPACE)
    both = lambda start: [
        pair for i in range(start, size - 1, 2) for pair in ((i, i + 1), (i + 1, i))
    ]
    cross = lambda pairs: [(2 * i + t, 2 * j + 1 - t) for i, j in pairs for t in (0, 1)]
    return (
        lax.ppermute(even_side, SPACE, both(0)),
        lax.ppermute(odd_side, SPACE, both(1)),
        swap(time, TIME),
        lax.ppermute(even_diag, (*SPACE, TIME), cross(both(0))),
        lax.ppermute(odd_diag, (*SPACE, TIME), cross(both(1))),
    )


def spread(value, axes):
    size = math.prod(lax.axis_size(axis) for axis in axes)
    copies = jnp.broadcast_to(value[None], (size, *value.shape))
    return lax.all_to_all(copies, axes, 0, 0)


def reduce_all(keep, send, scale, early):
    total = (keep + swap(send, "c").astype(F32)).astype(BF)
    total, early = lax.optimization_barrier((total, early))
    plane = math.prod(lax.axis_size(axis) for axis in PLANE)
    rows = 27 * CH // plane
    parts = lax.all_to_all(total.reshape(plane, rows, CH), PLANE, 0, 0)
    total = jnp.sum(parts.astype(F32), axis=0)
    depth = lax.axis_size("z")
    parts = lax.all_to_all(total.reshape(depth, rows // depth, CH), "z", 0, 0)
    total = (jnp.sum(parts, axis=0) * scale).astype(BF)
    total = spread(total, ("z",)).reshape(rows, CH)
    mine = spread(total, PLANE).reshape(27, CH, CH)
    mine, early = lax.optimization_barrier((mine, early))
    other = swap(mine, "c")
    even = lax.axis_index("c") == 0
    second = jnp.where(even, mine, other).astype(F32)
    first = jnp.where(even, other, mine).astype(F32)
    return first, second, early


def body(features, cotangent, w_first, w_second, occupancy, neighbors, send_space, send_time):
    f, g = (a.reshape(BLK, VOX, CH) for a in (features, cotangent))
    half = lax.axis_index(TIME).astype(jnp.int32).reshape(1)
    core = lax.axis_index("c").astype(jnp.int32).reshape(1)
    sends = send_space.reshape(2, BLK)
    table = neighbors.reshape(BLK, 27)
    when = send_time.reshape(2 * BLK)
    xg, mask, *messages = pack(f, g, occupancy.reshape(BLK, VOX), sends, when, half, core)
    halos = exchange(messages)
    gp, keep, send = local_pass(table, core, xg, mask, w_first, w_second, halos)
    early = input_grad(0, gp, mask, g, w_first)
    devices = math.prod(lax.axis_size(axis) for axis in (*SPACE, TIME))
    scale = 1.0 / math.sqrt(devices * ROWS)
    first, second, early = reduce_all(keep, send, scale, early)
    out = input_grad(1, gp, mask, g, w_first, early)
    return out.reshape(features.shape), first, second


def solution(mesh):
    fine = Mesh(
        mesh.devices.reshape(*SPLIT.values(), mesh.shape["tm"]), (*SPACE, TIME)
    )
    split = lambda rank: P(SPACE, TIME, *[None] * (rank - 2))
    return jax.shard_map(
        body,
        mesh=fine,
        in_specs=(
            split(5), split(5), P(), P(), split(4), split(4), split(4), split(3),
        ),
        out_specs=(split(5), P(), P()),
        check_vma=False,
    )
```

```python
import functools
import math

import jax
import jax.numpy as jnp
from jax import lax
from jax.experimental import pallas as pl
from jax.experimental.pallas import tpu as pltpu
from jax.sharding import Mesh
from jax.sharding import PartitionSpec as P

SPLIT = {"z": 8, "x": 4, "yh": 2, "c": 2}
SPACE = ("z", "x", "yh", "c")
TIME = "yl"
PLANE = ("x", "yh", "yl")

E = 8
CH = 128
FACE = E * E
VOX = E * FACE
BLK = 2
ROWS = BLK * VOX
RIM = 4 * FACE + 4 * E
BF = jnp.bfloat16
F32 = jnp.float32

WINDOWS = [(dt, dx) for dt in (-1, 0, 1) for dx in (-1, 0, 1)]

VM = pl.BlockSpec(memory_space=pltpu.VMEM)
SM = pl.BlockSpec(memory_space=pltpu.SMEM)
HB = pl.BlockSpec(memory_space=pltpu.HBM)
DMA = pltpu.SemaphoreType.DMA
I32 = jnp.int32
PARAMS = pltpu.CompilerParams(vmem_limit_bytes=32 * 1024 * 1024)


def stack_rows(parts):
    return jnp.concatenate([part.reshape(-1, CH) for part in parts], axis=0)


def load(sems, pairs):
    copies = [pltpu.make_async_copy(src, dst, sems.at[i]) for i, (src, dst) in enumerate(pairs)]
    for copy in copies:
        copy.start()
    return copies


def pack_kernel(half, core, f, g, occ, sends_in, when_in, xg_ref, mask_ref, *refs):
    even_ref, odd_ref, time_ref, even_diag, odd_diag, *scratch, sems = refs
    f_ref, g_ref, occ_ref, sends, when = scratch
    for copy in load(sems, list(zip((f, g, occ, sends_in, when_in), scratch))):
        copy.wait()
    even = core[0] == 0
    sides, times, corners = [], [], []
    for b in range(BLK):
        row = occ_ref[b : b + 1, :].astype(F32)
        mask = jnp.broadcast_to(row, (CH, VOX)).T
        mask_ref[b] = mask
        values = []
        for i, ref in enumerate((f_ref, g_ref)):
            masked = ref[b].astype(F32) * mask
            xg_ref[i, b] = masked.astype(BF)
            values.append(masked.reshape(E, FACE, CH))
        mask = mask.reshape(E, FACE, CH)
        low = stack_rows([v[:, : 2 * E] for v in values] + [mask[:, :E]])
        high = stack_rows([v[:, FACE - 2 * E :] for v in values] + [mask[:, FACE - E :]])
        sides.append((low, high))
        first = half[0] == 0
        edge = [jnp.where(first, v[E - 2 :], v[:2]) for v in values]
        edge.append(jnp.where(first, mask[E - 1 :], mask[:1]))
        times.append(stack_rows(edge))
        pad = jnp.zeros((E, CH), F32)
        low = stack_rows([v[:, : 2 * E] for v in edge[:2]] + [edge[2][:, :E], pad])
        high = stack_rows(
            [v[:, FACE - 2 * E :] for v in edge[:2]] + [edge[2][:, FACE - E :], pad]
        )
        corners.append((low, high))
    rows = lax.broadcasted_iota(jnp.int32, (2 * E, CH), 0)
    note = jnp.zeros((2 * E, CH), F32)
    for p in range(2 * BLK):
        note = jnp.where(rows == p, when[0, p].astype(F32), note)
    for side_ref, diag_ref, up in ((even_ref, even_diag, even), (odd_ref, odd_diag, ~even)):
        for slot in range(BLK):
            index = jnp.where(up, sends[1, slot], sends[0, slot])
            for ref, options in ((side_ref, sides), (diag_ref, corners)):
                value = jnp.zeros(options[0][0].shape, F32)
                for b, (low, high) in enumerate(options):
                    value = jnp.where(index == b, jnp.where(up, high, low), value)
                ref[slot] = value.astype(BF)
    for b in range(BLK):
        time_ref[b] = jnp.concatenate([times[b], note], axis=0).astype(BF)


def select(flag, value, other):
    if flag.ndim == 0:
        return jnp.where(flag, value, other)
    tiles = lambda v: v.reshape(-1, E, CH)
    chosen = jnp.where(jnp.broadcast_to(flag, tiles(value).shape), tiles(value), tiles(other))
    return chosen.reshape(value.shape)


def build(targets, owns, table, ready, even, halos):
    even_side, odd_side, across, even_diag, odd_diag = (
        [ref[j].astype(F32) for j in range(BLK)] for ref in halos
    )
    either = lambda a, b: [jnp.where(even, p, q) for p, q in zip(a, b)]
    below, below_diag = either(odd_side, even_side), either(odd_diag, even_diag)
    above, above_diag = either(even_side, odd_side), either(even_diag, odd_diag)
    notes = [
        jnp.broadcast_to(across[0][5 * FACE + p : 5 * FACE + p + 1], (E, CH))
        for p in range(2 * BLK)
    ]
    for (tile, w, _, _), own in zip(targets, owns):
        for b in range(BLK):
            tile[b, w : w + E, w * E : w * E + FACE] = own[b]
    ready()
    for b in range(BLK):
        for dt, dx in WINDOWS:
            if dt == 0 and dx == 0:
                continue
            slot = table[b, (dt + 1) * 9 + (dx + 1) * 3 + 1]
            side, diag = (below, below_diag) if dx < 0 else (above, above_diag)
            first = BLK if dx < 0 else 2 * BLK
            far = jnp.full((E, CH), -1.0, F32)
            for p, note in enumerate(notes):
                far = jnp.where(slot == 3 * BLK + p, note, far)
            for (tile, w, row, corner), own in zip(targets, owns):
                ts = {-1: slice(E - w, E), 0: slice(0, E), 1: slice(0, w)}[dt]
                xs = {-1: slice(FACE - w * E, FACE), 0: slice(0, FACE), 1: slice(0, w * E)}[dx]
                to_t = {-1: slice(0, w), 0: slice(w, w + E), 1: slice(w + E, 2 * w + E)}[dt]
                end = w * E + FACE
                to_x = {-1: slice(0, w * E), 0: slice(w * E, end), 1: slice(end, end + w * E)}[dx]
                value = jnp.zeros(own[0][ts, xs].shape, F32)
                for j in range(BLK):
                    value = select(slot == j, own[j][ts, xs], value)
                    if dx != 0:
                        face = side[j][row : row + FACE * w].reshape(E, w * E, CH)
                        value = select(slot == first + j, face[ts], value)
                    if dt != 0:
                        face = across[j][row : row + FACE * w].reshape(w, FACE, CH)
                        value = select(far == j, face[:, xs], value)
                    if dt != 0 and dx != 0:
                        face = diag[j][corner : corner + E * w * w].reshape(w, w * E, CH)
                        value = select(far == first + j, face, value)
                tile[b, to_t, to_x] = value


def pieces(tile, b, w, dt, dx):
    cut = lambda t, nt, x, nx: tile[
        b, w + t + dt : w + t + dt + nt, E * (w + x + dx) : E * (w + x + dx + nx)
    ].reshape(nt * nx * E, CH)
    rim = [(-1, 1, -1, E + 2), (E, 1, -1, E + 2), (0, E, -1, 1), (0, E, E, 1)]
    return cut(0, E, 0, E), lambda: [cut(*part) for part in rim]


def columns(tile, w, sign, cols, blocks, rim):
    for k, (dt, dx) in enumerate(WINDOWS):
        lane = slice(k * CH, (k + 1) * CH)
        for i, b in enumerate(blocks):
            core, ring = pieces(tile, b, w, sign * dt, sign * dx)
            cols[i * VOX : (i + 1) * VOX, lane] = core.astype(BF)
            if rim:
                at = ROWS + i * RIM
                cols[at : at + RIM, lane] = jnp.concatenate(ring(), axis=0).astype(BF)


def shift(value, step):
    y = lax.broadcasted_iota(jnp.int32, value.shape, 0) % E
    moved = pltpu.roll(value, (-step) % value.shape[0], 0)
    return jnp.where(y == (E - 1 if step > 0 else 0), 0.0, moved)


def lanes(value, dy):
    return value[:, (dy + 1) * CH : (dy + 2) * CH]


def gather_y(parts, sign):
    return lanes(parts, 0) + shift(lanes(parts, 1), sign) + shift(lanes(parts, -1), -sign)


def transposed(cols, w_ref, wide):
    for k in range(27):
        w, d = divmod(k, 3)
        wide[d * CH : (d + 1) * CH, w * CH : (w + 1) * CH] = w_ref[k]
    parts = lax.dot_general(
        cols[...], wide[...], (((1,), (1,)), ((), ())), preferred_element_type=F32
    )
    return gather_y(parts, -1)


def outer(left, right):
    return lax.dot_general(left, right, (((0,), (0,)), ((), ())), preferred_element_type=F32)


def local_kernel(
    core, xg, mask_ref, table_in, w1_in, w2_in, h0, h1, h2, h3, h4,
    gp_ref, keep_ref, send_ref,
    xtile, gtile, mtile, xcol, gcol, wide, tall, table, w1, w2, sems,
):
    copies = load(sems, [(table_in, table), (w1_in, w1), (w2_in, w2)])
    owns = [[xg[i, b].astype(F32).reshape(E, FACE, CH) for b in range(BLK)] for i in range(2)]
    owns.append([mask_ref[b].reshape(E, FACE, CH) for b in range(BLK)])
    targets = [
        (xtile, 2, 0, 0),
        (gtile, 2, 2 * FACE, 4 * E),
        (mtile, 1, 4 * FACE, 8 * E),
    ]
    even = core[0] == 0
    build(targets, owns, table, copies[0].wait, even, (h0, h1, h2, h3, h4))
    columns(xtile, 2, 1, xcol, range(BLK), True)
    columns(gtile, 2, -1, gcol, range(BLK), True)
    parts = [pieces(mtile, b, 1, 0, 0) for b in range(BLK)]
    mask = jnp.concatenate([p[0] for p in parts] + parts[0][1]() + parts[1][1](), axis=0)
    copies[1].wait()
    for k in range(27):
        w, d = divmod(k, 3)
        tall[w * CH : (w + 1) * CH, d * CH : (d + 1) * CH] = w1[k]
    parts = jnp.dot(xcol[...], tall[...], preferred_element_type=F32)
    pre = gather_y(parts, 1)
    sig = jax.nn.sigmoid(pre)
    hidden = (pre[:ROWS] * sig[:ROWS] * mask[:ROWS]).astype(BF).astype(F32)
    shifted = jnp.concatenate([shift(hidden, -1), hidden, shift(hidden, 1)], axis=1).astype(BF)
    second = outer(shifted, gcol[:ROWS])
    copies[2].wait()
    grad_hidden = transposed(gcol, w2, wide)
    grad_pre = (grad_hidden * sig * (1.0 + pre * (1.0 - sig)) * mask).astype(BF).astype(F32)
    for b in range(BLK):
        at = ROWS + b * RIM
        side = (E + 2) * E
        gp_ref[b, 1 : E + 1, E : E + FACE] = grad_pre[b * VOX : (b + 1) * VOX].reshape(E, FACE, CH)
        gp_ref[b, 0] = grad_pre[at : at + side]
        gp_ref[b, E + 1] = grad_pre[at + side : at + 2 * side]
        at += 2 * side
        gp_ref[b, 1 : E + 1, 0:E] = grad_pre[at : at + FACE].reshape(E, E, CH)
        gp_ref[b, 1 : E + 1, E + FACE :] = grad_pre[at + FACE : at + 2 * FACE].reshape(E, E, CH)
    grad_pre = grad_pre[:ROWS]
    shifted = jnp.concatenate(
        [shift(grad_pre, 1), grad_pre, shift(grad_pre, -1)], axis=1
    ).astype(BF)
    first = outer(xcol[:ROWS], shifted)
    for k in range(27):
        w, d = divmod(k, 3)
        a = second[d * CH : (d + 1) * CH, w * CH : (w + 1) * CH]
        b = first[w * CH : (w + 1) * CH, d * CH : (d + 1) * CH]
        keep_ref[k] = jnp.where(even, a, b)
        send_ref[k] = jnp.where(even, b, a).astype(BF)


def input_block(block, gp, mask_ref, cot, w1, dcol, wide):
    columns(gp, 1, -1, dcol, [block], False)
    total = transposed(dcol, w1, wide) * mask_ref[block]
    return (cot[block].astype(F32) + total).astype(BF)


def early_kernel(gp, mask_ref, cot, w1, out, dcol, wide):
    out[...] = input_block(0, gp, mask_ref, cot, w1, dcol, wide)


def to_half(core, mine, value, first, second, sem, act):
    even = (core[0] == 0) if mine else (core[0] != 0)
    for flag, target in ((even, second), (~even, first)):
        copy = pltpu.make_async_copy(value, target, sem)
        pl.when(flag)(copy.start if act == "start" else copy.wait)


def late_kernel(core, gp, mask_ref, cot, w1, early, mine, out, first, second, *scratch):
    dcol, wide, value, sem = scratch
    value[...] = mine[...].astype(F32)
    to_half(core, True, value, first, second, sem, "start")
    out[0] = early[...]
    out[1] = input_block(1, gp, mask_ref, cot, w1, dcol, wide)
    to_half(core, True, value, first, second, sem, "wait")


def last_kernel(core, other, first_in, second_in, first, second, value, sem):
    value[...] = other[...].astype(F32)
    to_half(core, False, value, first, second, sem, "start")
    to_half(core, False, value, first, second, sem, "wait")


def in_place(value):
    return pltpu.with_memory_space_constraint(value, pltpu.HBM)


def pack(f, g, occ, sends, when, half, core):
    shapes = [5 * FACE, 5 * FACE, 5 * FACE + 2 * E, 10 * E, 10 * E]
    return pl.pallas_call(
        pack_kernel,
        out_shape=[
            jax.ShapeDtypeStruct((2, BLK, VOX, CH), BF),
            jax.ShapeDtypeStruct((BLK, VOX, CH), F32),
            *[jax.ShapeDtypeStruct((BLK, rows, CH), BF) for rows in shapes],
        ],
        in_specs=[SM] * 2 + [HB] * 5,
        out_specs=[VM] * 7,
        scratch_shapes=[
            pltpu.VMEM((BLK, VOX, CH), BF),
            pltpu.VMEM((BLK, VOX, CH), BF),
            pltpu.VMEM((BLK, VOX), I32),
            pltpu.SMEM((2, BLK), I32),
            pltpu.SMEM((1, 2 * BLK), I32),
            DMA((5,)),
        ],
        compiler_params=PARAMS,
        name="pack",
    )(half, core, *map(in_place, (f, g, occ, sends, when)))


def local_pass(table, core, xg, mask, w1, w2, halos):
    return pl.pallas_call(
        local_kernel,
        out_shape=[
            jax.ShapeDtypeStruct((BLK, E + 2, (E + 2) * E, CH), F32),
            jax.ShapeDtypeStruct((27, CH, CH), F32),
            jax.ShapeDtypeStruct((27, CH, CH), BF),
        ],
        in_specs=[SM] + [VM] * 2 + [HB] * 3 + [VM] * 5,
        out_specs=[VM] * 3,
        scratch_shapes=[
            pltpu.VMEM((BLK, E + 4, (E + 4) * E, CH), F32),
            pltpu.VMEM((BLK, E + 4, (E + 4) * E, CH), F32),
            pltpu.VMEM((BLK, E + 2, (E + 2) * E, CH), F32),
            pltpu.VMEM((ROWS + BLK * RIM, 9 * CH), BF),
            pltpu.VMEM((ROWS + BLK * RIM, 9 * CH), BF),
            pltpu.VMEM((3 * CH, 9 * CH), BF),
            pltpu.VMEM((9 * CH, 3 * CH), BF),
            pltpu.SMEM((BLK, 27), I32),
            pltpu.VMEM((27, CH, CH), BF),
            pltpu.VMEM((27, CH, CH), BF),
            DMA((3,)),
        ],
        compiler_params=PARAMS,
        name="local_pass",
    )(core, xg, mask, *map(in_place, (table, w1, w2)), *halos)


INPUT_SCRATCH = [pltpu.VMEM((VOX, 9 * CH), BF), pltpu.VMEM((3 * CH, 9 * CH), BF)]
HALF_SCRATCH = [pltpu.VMEM((27, CH, CH), F32), DMA(())]


def early_grad(gp, mask, cot, w1):
    return pl.pallas_call(
        early_kernel,
        out_shape=jax.ShapeDtypeStruct((VOX, CH), BF),
        in_specs=[VM] * 4,
        out_specs=VM,
        scratch_shapes=INPUT_SCRATCH,
        compiler_params=PARAMS,
        name="early_grad",
    )(gp, mask, cot, w1)


def late_grad(core, gp, mask, cot, w1, early, mine):
    weights = jax.ShapeDtypeStruct((27, CH, CH), F32)
    return pl.pallas_call(
        late_kernel,
        out_shape=[jax.ShapeDtypeStruct((BLK, VOX, CH), BF), weights, weights],
        in_specs=[SM] + [VM] * 6,
        out_specs=[VM, HB, HB],
        scratch_shapes=INPUT_SCRATCH + HALF_SCRATCH,
        compiler_params=PARAMS,
        name="late_grad",
    )(core, gp, mask, cot, w1, early, mine)


def last_half(core, other, first, second):
    weights = jax.ShapeDtypeStruct((27, CH, CH), F32)
    return pl.pallas_call(
        last_kernel,
        out_shape=[weights, weights],
        in_specs=[SM, VM, HB, HB],
        out_specs=[HB, HB],
        scratch_shapes=HALF_SCRATCH,
        input_output_aliases={2: 0, 3: 1},
        compiler_params=PARAMS,
        name="last_half",
    )(core, other, first, second)


def swap(value, axis):
    return lax.ppermute(value, axis, [(0, 1), (1, 0)])


def exchange(messages):
    even_side, odd_side, time, even_diag, odd_diag = messages
    size = math.prod(lax.axis_size(axis) for axis in SPACE)
    both = lambda start: [
        pair for i in range(start, size - 1, 2) for pair in ((i, i + 1), (i + 1, i))
    ]
    cross = lambda pairs: [(2 * i + t, 2 * j + 1 - t) for i, j in pairs for t in (0, 1)]
    return (
        lax.ppermute(even_side, SPACE, both(0)),
        lax.ppermute(odd_side, SPACE, both(1)),
        swap(time, TIME),
        lax.ppermute(even_diag, (*SPACE, TIME), cross(both(0))),
        lax.ppermute(odd_diag, (*SPACE, TIME), cross(both(1))),
    )


def spread(value, axes):
    size = math.prod(lax.axis_size(axis) for axis in axes)
    copies = jnp.broadcast_to(value[None], (size, *value.shape))
    return lax.all_to_all(copies, axes, 0, 0)


def reduce_all(keep, send, scale, early):
    total = (keep + swap(send, "c").astype(F32)).astype(BF)
    total, early = lax.optimization_barrier((total, early))
    plane = math.prod(lax.axis_size(axis) for axis in PLANE)
    rows = 27 * CH // plane
    parts = lax.all_to_all(total.reshape(plane, rows, CH), PLANE, 0, 0)
    total = jnp.sum(parts.astype(F32), axis=0)
    depth = lax.axis_size("z")
    parts = lax.all_to_all(total.reshape(depth, rows // depth, CH), "z", 0, 0)
    total = (jnp.sum(parts, axis=0) * scale).astype(BF)
    total = spread(total, ("z",)).reshape(rows, CH)
    mine = spread(total, PLANE).reshape(27, CH, CH)
    mine, early = lax.optimization_barrier((mine, early))
    return mine, swap(mine, "c"), early


def body(features, cotangent, w_first, w_second, occupancy, neighbors, send_space, send_time):
    f, g = (a.reshape(BLK, VOX, CH) for a in (features, cotangent))
    half = lax.axis_index(TIME).astype(jnp.int32).reshape(1)
    core = lax.axis_index("c").astype(jnp.int32).reshape(1)
    sends = send_space.reshape(2, BLK)
    table = neighbors.reshape(BLK, 27)
    when = send_time.reshape(1, 2 * BLK)
    xg, mask, *messages = pack(f, g, occupancy.reshape(BLK, VOX), sends, when, half, core)
    halos = exchange(messages)
    gp, keep, send = local_pass(table, core, xg, mask, w_first, w_second, halos)
    early = early_grad(gp, mask, g, w_first)
    devices = math.prod(lax.axis_size(axis) for axis in (*SPACE, TIME))
    scale = 1.0 / math.sqrt(devices * ROWS)
    mine, other, early = reduce_all(keep, send, scale, early)
    out, first, second = late_grad(core, gp, mask, g, w_first, early, mine)
    first, second = last_half(core, other, first, second)
    return out.reshape(features.shape), first, second


def solution(mesh):
    fine = Mesh(
        mesh.devices.reshape(*SPLIT.values(), mesh.shape["tm"]), (*SPACE, TIME)
    )
    split = lambda rank: P(SPACE, TIME, *[None] * (rank - 2))
    return jax.shard_map(
        body,
        mesh=fine,
        in_specs=(
            split(5), split(5), P(), P(), split(4), split(4), split(4), split(3),
        ),
        out_specs=(split(5), P(), P()),
        check_vma=False,
    )
```

```python
import functools
import math

import jax
import jax.numpy as jnp
from jax import lax
from jax.experimental import pallas as pl
from jax.experimental.pallas import tpu as pltpu
from jax.sharding import Mesh
from jax.sharding import PartitionSpec as P

SPLIT = {"z": 8, "x": 4, "yh": 2, "c": 2}
SPACE = ("z", "x", "yh", "c")
TIME = "yl"
PLANE = ("x", "yh", "yl")

E = 8
CH = 128
FACE = E * E
VOX = E * FACE
BLK = 2
ROWS = BLK * VOX
INNER = [(1, E - 2, 1, E - 2)]
OWN = [(0, 1, 0, E), (E - 1, 1, 0, E), (1, E - 2, 0, 1), (1, E - 2, E - 1, 1)]
RIM = [(-1, 1, -1, E + 2), (E, 1, -1, E + 2), (0, E, -1, 1), (0, E, E, 1)]
ALL = [(0, E, 0, E)]
EACH = range(BLK)
BF = jnp.bfloat16
F32 = jnp.float32

WINDOWS = [(dt, dx) for dt in (-1, 0, 1) for dx in (-1, 0, 1)]

VM = pl.BlockSpec(memory_space=pltpu.VMEM)
SM = pl.BlockSpec(memory_space=pltpu.SMEM)
HB = pl.BlockSpec(memory_space=pltpu.HBM)
DMA = pltpu.SemaphoreType.DMA
I32 = jnp.int32
PARAMS = pltpu.CompilerParams(vmem_limit_bytes=32 * 1024 * 1024)


def stack_rows(parts):
    return jnp.concatenate([part.reshape(-1, CH) for part in parts], axis=0)


def load(sems, pairs):
    copies = [pltpu.make_async_copy(src, dst, sems.at[i]) for i, (src, dst) in enumerate(pairs)]
    for copy in copies:
        copy.start()
    return copies


def pack_kernel(half, core, f, g, occ, sends_in, when_in, xg_ref, mask_ref, *refs):
    even_ref, odd_ref, time_ref, even_diag, odd_diag, *scratch, sems = refs
    f_ref, g_ref, occ_ref, sends, when = scratch
    for copy in load(sems, list(zip((f, g, occ, sends_in, when_in), scratch))):
        copy.wait()
    even = core[0] == 0
    sides, times, corners = [], [], []
    for b in range(BLK):
        row = occ_ref[b : b + 1, :].astype(F32)
        mask = jnp.broadcast_to(row, (CH, VOX)).T
        mask_ref[b] = mask.reshape(E, FACE, CH)
        values = []
        for i, ref in enumerate((f_ref, g_ref)):
            masked = ref[b].astype(F32) * mask
            masked = masked.reshape(E, FACE, CH)
            xg_ref[i, b] = masked.astype(BF)
            values.append(masked)
        mask = mask.reshape(E, FACE, CH)
        low = stack_rows([v[:, : 2 * E] for v in values] + [mask[:, :E]])
        high = stack_rows([v[:, FACE - 2 * E :] for v in values] + [mask[:, FACE - E :]])
        sides.append((low, high))
        first = half[0] == 0
        edge = [jnp.where(first, v[E - 2 :], v[:2]) for v in values]
        edge.append(jnp.where(first, mask[E - 1 :], mask[:1]))
        times.append(stack_rows(edge))
        pad = jnp.zeros((E, CH), F32)
        low = stack_rows([v[:, : 2 * E] for v in edge[:2]] + [edge[2][:, :E], pad])
        high = stack_rows(
            [v[:, FACE - 2 * E :] for v in edge[:2]] + [edge[2][:, FACE - E :], pad]
        )
        corners.append((low, high))
    rows = lax.broadcasted_iota(jnp.int32, (2 * E, CH), 0)
    note = jnp.zeros((2 * E, CH), F32)
    for p in range(2 * BLK):
        note = jnp.where(rows == p, when[0, p].astype(F32), note)
    for side_ref, diag_ref, up in ((even_ref, even_diag, even), (odd_ref, odd_diag, ~even)):
        for slot in range(BLK):
            index = jnp.where(up, sends[1, slot], sends[0, slot])
            for ref, options in ((side_ref, sides), (diag_ref, corners)):
                value = jnp.zeros(options[0][0].shape, F32)
                for b, (low, high) in enumerate(options):
                    value = jnp.where(index == b, jnp.where(up, high, low), value)
                ref[slot] = value.astype(BF)
    for b in range(BLK):
        time_ref[b] = jnp.concatenate([times[b], note], axis=0).astype(BF)


def select(flag, value, other):
    if flag.ndim == 0:
        return jnp.where(flag, value, other)
    tiles = lambda v: v.reshape(-1, E, CH)
    chosen = jnp.where(jnp.broadcast_to(flag, tiles(value).shape), tiles(value), tiles(other))
    return chosen.reshape(value.shape)


def build(targets, owns, table, ready, even, halos):
    even_side, odd_side, across, even_diag, odd_diag = (
        [ref[j].astype(F32) for j in range(BLK)] for ref in halos
    )
    either = lambda a, b: [jnp.where(even, p, q) for p, q in zip(a, b)]
    below, below_diag = either(odd_side, even_side), either(odd_diag, even_diag)
    above, above_diag = either(even_side, odd_side), either(even_diag, odd_diag)
    notes = [
        jnp.broadcast_to(across[0][5 * FACE + p : 5 * FACE + p + 1], (E, CH))
        for p in range(2 * BLK)
    ]
    for (tile, w, _, _), own in zip(targets, owns):
        for b in range(BLK):
            tile[b, w : w + E, w * E : w * E + FACE] = own[b]
    ready()
    for b in range(BLK):
        for dt, dx in WINDOWS:
            if dt == 0 and dx == 0:
                continue
            slot = table[b, (dt + 1) * 9 + (dx + 1) * 3 + 1]
            side, diag = (below, below_diag) if dx < 0 else (above, above_diag)
            first = BLK if dx < 0 else 2 * BLK
            far = jnp.full((E, CH), -1.0, F32)
            for p, note in enumerate(notes):
                far = jnp.where(slot == 3 * BLK + p, note, far)
            for (tile, w, row, corner), own in zip(targets, owns):
                ts = {-1: slice(E - w, E), 0: slice(0, E), 1: slice(0, w)}[dt]
                xs = {-1: slice(FACE - w * E, FACE), 0: slice(0, FACE), 1: slice(0, w * E)}[dx]
                to_t = {-1: slice(0, w), 0: slice(w, w + E), 1: slice(w + E, 2 * w + E)}[dt]
                end = w * E + FACE
                to_x = {-1: slice(0, w * E), 0: slice(w * E, end), 1: slice(end, end + w * E)}[dx]
                value = jnp.zeros(own[0][ts, xs].shape, F32)
                for j in range(BLK):
                    value = select(slot == j, own[j][ts, xs], value)
                    if dx != 0:
                        face = side[j][row : row + FACE * w].reshape(E, w * E, CH)
                        value = select(slot == first + j, face[ts], value)
                    if dt != 0:
                        face = across[j][row : row + FACE * w].reshape(w, FACE, CH)
                        value = select(far == j, face[:, xs], value)
                    if dt != 0 and dx != 0:
                        face = diag[j][corner : corner + E * w * w].reshape(w, w * E, CH)
                        value = select(far == first + j, face, value)
                tile[b, to_t, to_x] = value


def size(part):
    return part[1] * part[3] * E


def span(part, w, dt=0, dx=0):
    t, nt, x, nx = part
    return (
        slice(w + t + dt, w + t + dt + nt),
        slice(E * (w + x + dx), E * (w + x + dx + nx)),
    )


def cut(tile, w, groups, dt=0, dx=0):
    return [
        tile[(b, *span(part, w, dt, dx))].reshape(size(part), CH)
        for b, parts in groups
        for part in parts
    ]


def columns(tile, w, sign, cols, groups):
    for k, (dt, dx) in enumerate(WINDOWS):
        rows = jnp.concatenate(cut(tile, w, groups, sign * dt, sign * dx), axis=0)
        cols[:, k * CH : (k + 1) * CH] = rows.astype(BF)


def shift(value, step):
    y = lax.broadcasted_iota(jnp.int32, value.shape, 0) % E
    moved = pltpu.roll(value, (-step) % value.shape[0], 0)
    return jnp.where(y == (E - 1 if step > 0 else 0), 0.0, moved)


def lanes(value, dy):
    return value[:, (dy + 1) * CH : (dy + 2) * CH]


def gather_y(parts, sign):
    return lanes(parts, 0) + shift(lanes(parts, 1), sign) + shift(lanes(parts, -1), -sign)


def transposed(cols, wide):
    parts = lax.dot_general(
        cols[...], wide[...], (((1,), (1,)), ((), ())), preferred_element_type=F32
    )
    return gather_y(parts, -1)


def arrange(w_ref, tall, wide):
    for k in range(27):
        w, d = divmod(k, 3)
        if tall is not None:
            tall[w * CH : (w + 1) * CH, d * CH : (d + 1) * CH] = w_ref[k]
        if wide is not None:
            wide[d * CH : (d + 1) * CH, w * CH : (w + 1) * CH] = w_ref[k]


def outer(left, right):
    return lax.dot_general(left, right, (((0,), (0,)), ((), ())), preferred_element_type=F32)


def local_math(xcol, gcol, mask, tall, wide, own):
    pre = gather_y(jnp.dot(xcol[...], tall[...], preferred_element_type=F32), 1)
    sig = jax.nn.sigmoid(pre)
    hidden = (pre[:own] * sig[:own] * mask[:own]).astype(BF).astype(F32)
    shifted = jnp.concatenate([shift(hidden, -1), hidden, shift(hidden, 1)], axis=1).astype(BF)
    second = outer(shifted, gcol[:own])
    grad_hidden = transposed(gcol, wide)
    grad_pre = (grad_hidden * sig * (1.0 + pre * (1.0 - sig)) * mask).astype(BF).astype(F32)
    mine = grad_pre[:own]
    shifted = jnp.concatenate([shift(mine, 1), mine, shift(mine, -1)], axis=1).astype(BF)
    first = outer(xcol[:own], shifted)
    return grad_pre, first, second


def inner_kernel(
    xg, mask_ref, w1_in, w2_in, gp_ref, first_ref, second_ref, tall, wide1, wide2,
    xtile, gtile, xcol, gcol, w1, w2, sems,
):
    copies = load(sems, [(w1_in, w1), (w2_in, w2)])
    groups = [(b, INNER) for b in EACH]
    xtile[...] = xg[0].astype(F32)
    gtile[...] = xg[1].astype(F32)
    columns(xtile, 0, 1, xcol, groups)
    columns(gtile, 0, -1, gcol, groups)
    mask = jnp.concatenate(cut(mask_ref, 0, groups), axis=0)
    for copy in copies:
        copy.wait()
    arrange(w1, tall, wide1)
    arrange(w2, None, wide2)
    rows = BLK * size(INNER[0])
    grad_pre, first, second = local_math(xcol, gcol, mask, tall, wide2, rows)
    first_ref[...] = first
    second_ref[...] = second
    gp_ref[...] = grad_pre.reshape(gp_ref.shape)


def outer_kernel(
    core, xg, mask_ref, table_in, tall, wide2, inner, first_in, second_in, h0, h1, h2, h3, h4,
    gp_ref, keep_ref, send_ref, xtile, gtile, mtile, xcol, gcol, table, sems,
):
    copies = load(sems, [(table_in, table)])
    owns = [[xg[i, b].astype(F32) for b in EACH] for i in range(2)]
    owns.append([mask_ref[b] for b in EACH])
    targets = [
        (xtile, 2, 0, 0),
        (gtile, 2, 2 * FACE, 4 * E),
        (mtile, 1, 4 * FACE, 8 * E),
    ]
    even = core[0] == 0
    build(targets, owns, table, copies[0].wait, even, (h0, h1, h2, h3, h4))
    groups = [(b, OWN) for b in EACH] + [(b, RIM) for b in EACH]
    columns(xtile, 2, 1, xcol, groups)
    columns(gtile, 2, -1, gcol, groups)
    mask = jnp.concatenate(cut(mtile, 1, groups), axis=0)
    rows = BLK * sum(size(part) for part in OWN)
    grad_pre, first, second = local_math(xcol, gcol, mask, tall, wide2, rows)
    at = 0
    for b, parts in groups:
        for part in parts:
            rows = grad_pre[at : at + size(part)].reshape(part[1], part[3] * E, CH)
            gp_ref[(b, *span(part, 1))] = rows
            at += size(part)
    for b in EACH:
        gp_ref[(b, *span(INNER[0], 1))] = inner[b]
    for k in range(27):
        w, d = divmod(k, 3)
        ws, ds = slice(w * CH, (w + 1) * CH), slice(d * CH, (d + 1) * CH)
        a = second[ds, ws] + second_in[ds, ws]
        b = first[ws, ds] + first_in[ws, ds]
        keep_ref[k] = jnp.where(even, a, b)
        send_ref[k] = jnp.where(even, b, a).astype(BF)


def grad_kernel(gp, mask_ref, cot, wide, out, dcol):
    columns(gp, 1, -1, dcol, [(b, ALL) for b in EACH])
    total = transposed(dcol, wide) * mask_ref[...].reshape(ROWS, CH)
    total = cot[...].astype(F32).reshape(ROWS, CH) + total
    out[...] = total.astype(BF).reshape(BLK, VOX, CH)


def to_half(core, mine, value, first, second, sem, act):
    even = (core[0] == 0) if mine else (core[0] != 0)
    for flag, target in ((even, second), (~even, first)):
        copy = pltpu.make_async_copy(value, target, sem)
        pl.when(flag)(copy.start if act == "start" else copy.wait)


def mine_kernel(core, mine, first, second, value, sem):
    value[...] = mine[...].astype(F32)
    to_half(core, True, value, first, second, sem, "start")
    to_half(core, True, value, first, second, sem, "wait")


def last_kernel(core, other, first_in, second_in, first, second, value, sem):
    value[...] = other[...].astype(F32)
    to_half(core, False, value, first, second, sem, "start")
    to_half(core, False, value, first, second, sem, "wait")


def in_place(value):
    return pltpu.with_memory_space_constraint(value, pltpu.HBM)


def pack(f, g, occ, sends, when, half, core):
    shapes = [5 * FACE, 5 * FACE, 5 * FACE + 2 * E, 10 * E, 10 * E]
    return pl.pallas_call(
        pack_kernel,
        out_shape=[
            jax.ShapeDtypeStruct((2, BLK, E, FACE, CH), BF),
            jax.ShapeDtypeStruct((BLK, E, FACE, CH), F32),
            *[jax.ShapeDtypeStruct((BLK, rows, CH), BF) for rows in shapes],
        ],
        in_specs=[SM] * 2 + [HB] * 5,
        out_specs=[VM] * 7,
        scratch_shapes=[
            pltpu.VMEM((BLK, VOX, CH), BF),
            pltpu.VMEM((BLK, VOX, CH), BF),
            pltpu.VMEM((BLK, VOX), I32),
            pltpu.SMEM((2, BLK), I32),
            pltpu.SMEM((1, 2 * BLK), I32),
            DMA((5,)),
        ],
        compiler_params=PARAMS,
        name="pack",
    )(half, core, *map(in_place, (f, g, occ, sends, when)))


def inner_pass(xg, mask, w1, w2):
    rows = BLK * size(INNER[0])
    tall, wide = (9 * CH, 3 * CH), (3 * CH, 9 * CH)
    return pl.pallas_call(
        inner_kernel,
        out_shape=[
            jax.ShapeDtypeStruct((BLK, E - 2, (E - 2) * E, CH), F32),
            jax.ShapeDtypeStruct(tall, F32),
            jax.ShapeDtypeStruct(wide, F32),
            jax.ShapeDtypeStruct(tall, BF),
            jax.ShapeDtypeStruct(wide, BF),
            jax.ShapeDtypeStruct(wide, BF),
        ],
        in_specs=[VM] * 2 + [HB] * 2,
        out_specs=[VM] * 6,
        scratch_shapes=[
            pltpu.VMEM((BLK, E, FACE, CH), F32),
            pltpu.VMEM((BLK, E, FACE, CH), F32),
            pltpu.VMEM((rows, 9 * CH), BF),
            pltpu.VMEM((rows, 9 * CH), BF),
            pltpu.VMEM((27, CH, CH), BF),
            pltpu.VMEM((27, CH, CH), BF),
            DMA((2,)),
        ],
        compiler_params=PARAMS,
        name="inner_pass",
    )(xg, mask, *map(in_place, (w1, w2)))


def outer_pass(core, xg, mask, table, tall, wide2, inner, first, second, halos):
    rows = BLK * sum(size(part) for part in OWN + RIM)
    return pl.pallas_call(
        outer_kernel,
        out_shape=[
            jax.ShapeDtypeStruct((BLK, E + 2, (E + 2) * E, CH), F32),
            jax.ShapeDtypeStruct((27, CH, CH), F32),
            jax.ShapeDtypeStruct((27, CH, CH), BF),
        ],
        in_specs=[SM] + [VM] * 2 + [HB] + [VM] * 10,
        out_specs=[VM] * 3,
        scratch_shapes=[
            pltpu.VMEM((BLK, E + 4, (E + 4) * E, CH), F32),
            pltpu.VMEM((BLK, E + 4, (E + 4) * E, CH), F32),
            pltpu.VMEM((BLK, E + 2, (E + 2) * E, CH), F32),
            pltpu.VMEM((rows, 9 * CH), BF),
            pltpu.VMEM((rows, 9 * CH), BF),
            pltpu.SMEM((BLK, 27), I32),
            DMA((1,)),
        ],
        compiler_params=PARAMS,
        name="outer_pass",
    )(core, xg, mask, in_place(table), tall, wide2, inner, first, second, *halos)


def input_grad(gp, mask, cot, wide):
    return pl.pallas_call(
        grad_kernel,
        out_shape=jax.ShapeDtypeStruct((BLK, VOX, CH), BF),
        in_specs=[VM] * 4,
        out_specs=VM,
        scratch_shapes=[pltpu.VMEM((ROWS, 9 * CH), BF)],
        compiler_params=PARAMS,
        name="input_grad",
    )(gp, mask, cot, wide)


HALF_SCRATCH = [pltpu.VMEM((27, CH, CH), F32), DMA(())]


def mine_half(core, mine):
    weights = jax.ShapeDtypeStruct((27, CH, CH), F32)
    return pl.pallas_call(
        mine_kernel,
        out_shape=[weights, weights],
        in_specs=[SM, VM],
        out_specs=[HB, HB],
        scratch_shapes=HALF_SCRATCH,
        compiler_params=PARAMS,
        name="mine_half",
    )(core, mine)


def last_half(core, other, first, second):
    weights = jax.ShapeDtypeStruct((27, CH, CH), F32)
    return pl.pallas_call(
        last_kernel,
        out_shape=[weights, weights],
        in_specs=[SM, VM, HB, HB],
        out_specs=[HB, HB],
        scratch_shapes=HALF_SCRATCH,
        input_output_aliases={2: 0, 3: 1},
        compiler_params=PARAMS,
        name="last_half",
    )(core, other, first, second)


def swap(value, axis):
    return lax.ppermute(value, axis, [(0, 1), (1, 0)])


def exchange(messages):
    even_side, odd_side, time, even_diag, odd_diag = messages
    size = math.prod(lax.axis_size(axis) for axis in SPACE)
    both = lambda start: [
        pair for i in range(start, size - 1, 2) for pair in ((i, i + 1), (i + 1, i))
    ]
    cross = lambda pairs: [(2 * i + t, 2 * j + 1 - t) for i, j in pairs for t in (0, 1)]
    return (
        lax.ppermute(even_side, SPACE, both(0)),
        lax.ppermute(odd_side, SPACE, both(1)),
        swap(time, TIME),
        lax.ppermute(even_diag, (*SPACE, TIME), cross(both(0))),
        lax.ppermute(odd_diag, (*SPACE, TIME), cross(both(1))),
    )


def spread(value, axes):
    size = math.prod(lax.axis_size(axis) for axis in axes)
    copies = jnp.broadcast_to(value[None], (size, *value.shape))
    return lax.all_to_all(copies, axes, 0, 0)


def reduce_all(keep, send, scale, early):
    total = (keep + swap(send, "c").astype(F32)).astype(BF)
    total, early = lax.optimization_barrier((total, early))
    plane = math.prod(lax.axis_size(axis) for axis in PLANE)
    rows = 27 * CH // plane
    parts = lax.all_to_all(total.reshape(plane, rows, CH), PLANE, 0, 0)
    total = jnp.sum(parts.astype(F32), axis=0)
    depth = lax.axis_size("z")
    parts = lax.all_to_all(total.reshape(depth, rows // depth, CH), "z", 0, 0)
    total = (jnp.sum(parts, axis=0) * scale).astype(BF)
    total = spread(total, ("z",)).reshape(rows, CH)
    mine = spread(total, PLANE).reshape(27, CH, CH)
    return mine, swap(mine, "c"), early


def body(features, cotangent, w_first, w_second, occupancy, neighbors, send_space, send_time):
    f, g = (a.reshape(BLK, VOX, CH) for a in (features, cotangent))
    half = lax.axis_index(TIME).astype(jnp.int32).reshape(1)
    core = lax.axis_index("c").astype(jnp.int32).reshape(1)
    sends = send_space.reshape(2, BLK)
    table = neighbors.reshape(BLK, 27)
    when = send_time.reshape(1, 2 * BLK)
    xg, mask, *messages = pack(f, g, occupancy.reshape(BLK, VOX), sends, when, half, core)
    halos = exchange(messages)
    inner, first, second, tall, wide1, wide2 = inner_pass(xg, mask, w_first, w_second)
    gp, keep, send = outer_pass(
        core, xg, mask, table, tall, wide2, inner, first, second, halos
    )
    out = input_grad(gp, mask, g, wide1)
    devices = math.prod(lax.axis_size(axis) for axis in (*SPACE, TIME))
    scale = 1.0 / math.sqrt(devices * ROWS)
    mine, other, out = reduce_all(keep, send, scale, out)
    first, second = mine_half(core, mine)
    first, second = last_half(core, other, first, second)
    return out.reshape(features.shape), first, second


def solution(mesh):
    fine = Mesh(
        mesh.devices.reshape(*SPLIT.values(), mesh.shape["tm"]), (*SPACE, TIME)
    )
    split = lambda rank: P(SPACE, TIME, *[None] * (rank - 2))
    return jax.shard_map(
        body,
        mesh=fine,
        in_specs=(
            split(5), split(5), P(), P(), split(4), split(4), split(4), split(3),
        ),
        out_specs=(split(5), P(), P()),
        check_vma=False,
    )
```

```python
import functools
import math

import jax
import jax.numpy as jnp
from jax import lax
from jax.experimental import pallas as pl
from jax.experimental.pallas import tpu as pltpu
from jax.sharding import Mesh
from jax.sharding import PartitionSpec as P

SPLIT = {"z": 8, "x": 4, "yh": 2, "c": 2}
SPACE = ("z", "x", "yh", "c")
TIME = "yl"
PLANE = ("x", "yh", "yl")

E = 8
CH = 128
FACE = E * E
VOX = E * FACE
BLK = 2
ROWS = BLK * VOX
INNER = [(1, E - 2, 1, E - 2)]
OWN = [(0, 1, 0, E), (E - 1, 1, 0, E), (1, E - 2, 0, 1), (1, E - 2, E - 1, 1)]
RIM = [(-1, 1, -1, E + 2), (E, 1, -1, E + 2), (0, E, -1, 1), (0, E, E, 1)]
ALL = [(0, E, 0, E)]
EACH = range(BLK)
BF = jnp.bfloat16
F32 = jnp.float32

WINDOWS = [(dt, dx) for dt in (-1, 0, 1) for dx in (-1, 0, 1)]

VM = pl.BlockSpec(memory_space=pltpu.VMEM)
SM = pl.BlockSpec(memory_space=pltpu.SMEM)
HB = pl.BlockSpec(memory_space=pltpu.HBM)
DMA = pltpu.SemaphoreType.DMA
I32 = jnp.int32
PARAMS = pltpu.CompilerParams(vmem_limit_bytes=32 * 1024 * 1024)


def stack_rows(parts):
    return jnp.concatenate([part.reshape(-1, CH) for part in parts], axis=0)


def load(sems, pairs):
    copies = [pltpu.make_async_copy(src, dst, sems.at[i]) for i, (src, dst) in enumerate(pairs)]
    for copy in copies:
        copy.start()
    return copies


def pack_kernel(half, core, f, g, occ, sends_in, when_in, xg_ref, mask_ref, *refs):
    even_ref, odd_ref, time_ref, even_diag, odd_diag, *scratch, sems = refs
    f_ref, g_ref, occ_ref, sends, when = scratch
    copies = load(sems, list(zip((f, g, occ, sends_in, when_in), scratch)))
    even = core[0] == 0
    sides, times, corners, masks = [], [], [], []
    copies[2].wait()
    for b in range(BLK):
        row = occ_ref[b : b + 1, :].astype(F32)
        masks.append(jnp.broadcast_to(row, (CH, VOX)).T)
        mask_ref[b] = masks[b].reshape(E, FACE, CH)
    for copy in copies[:2] + copies[3:]:
        copy.wait()
    for b in range(BLK):
        mask = masks[b]
        values = []
        for i, ref in enumerate((f_ref, g_ref)):
            masked = ref[b].astype(F32) * mask
            masked = masked.reshape(E, FACE, CH)
            xg_ref[i, b] = masked.astype(BF)
            values.append(masked)
        mask = mask.reshape(E, FACE, CH)
        low = stack_rows([v[:, : 2 * E] for v in values] + [mask[:, :E]])
        high = stack_rows([v[:, FACE - 2 * E :] for v in values] + [mask[:, FACE - E :]])
        sides.append((low, high))
        first = half[0] == 0
        edge = [jnp.where(first, v[E - 2 :], v[:2]) for v in values]
        edge.append(jnp.where(first, mask[E - 1 :], mask[:1]))
        times.append(stack_rows(edge))
        pad = jnp.zeros((E, CH), F32)
        low = stack_rows([v[:, : 2 * E] for v in edge[:2]] + [edge[2][:, :E], pad])
        high = stack_rows(
            [v[:, FACE - 2 * E :] for v in edge[:2]] + [edge[2][:, FACE - E :], pad]
        )
        corners.append((low, high))
    rows = lax.broadcasted_iota(jnp.int32, (2 * E, CH), 0)
    note = jnp.zeros((2 * E, CH), F32)
    for p in range(2 * BLK):
        note = jnp.where(rows == p, when[0, p].astype(F32), note)
    for side_ref, diag_ref, up in ((even_ref, even_diag, even), (odd_ref, odd_diag, ~even)):
        for slot in range(BLK):
            index = jnp.where(up, sends[1, slot], sends[0, slot])
            for ref, options in ((side_ref, sides), (diag_ref, corners)):
                value = jnp.zeros(options[0][0].shape, F32)
                for b, (low, high) in enumerate(options):
                    value = jnp.where(index == b, jnp.where(up, high, low), value)
                ref[slot] = value.astype(BF)
    for b in range(BLK):
        time_ref[b] = jnp.concatenate([times[b], note], axis=0).astype(BF)


def select(flag, value, other):
    if flag.ndim == 0:
        return jnp.where(flag, value, other)
    tiles = lambda v: v.reshape(-1, E, CH)
    chosen = jnp.where(jnp.broadcast_to(flag, tiles(value).shape), tiles(value), tiles(other))
    return chosen.reshape(value.shape)


def build(targets, owns, table, ready, even, halos):
    even_side, odd_side, across, even_diag, odd_diag = (
        [ref[j].astype(F32) for j in range(BLK)] for ref in halos
    )
    either = lambda a, b: [jnp.where(even, p, q) for p, q in zip(a, b)]
    below, below_diag = either(odd_side, even_side), either(odd_diag, even_diag)
    above, above_diag = either(even_side, odd_side), either(even_diag, odd_diag)
    notes = [
        jnp.broadcast_to(across[0][5 * FACE + p : 5 * FACE + p + 1], (E, CH))
        for p in range(2 * BLK)
    ]
    for (tile, w, _, _), own in zip(targets, owns):
        for b in range(BLK):
            tile[b, w : w + E, w * E : w * E + FACE] = own[b]
    ready()
    for b in range(BLK):
        for dt, dx in WINDOWS:
            if dt == 0 and dx == 0:
                continue
            slot = table[b, (dt + 1) * 9 + (dx + 1) * 3 + 1]
            side, diag = (below, below_diag) if dx < 0 else (above, above_diag)
            first = BLK if dx < 0 else 2 * BLK
            far = jnp.full((E, CH), -1.0, F32)
            for p, note in enumerate(notes):
                far = jnp.where(slot == 3 * BLK + p, note, far)
            for (tile, w, row, corner), own in zip(targets, owns):
                ts = {-1: slice(E - w, E), 0: slice(0, E), 1: slice(0, w)}[dt]
                xs = {-1: slice(FACE - w * E, FACE), 0: slice(0, FACE), 1: slice(0, w * E)}[dx]
                to_t = {-1: slice(0, w), 0: slice(w, w + E), 1: slice(w + E, 2 * w + E)}[dt]
                end = w * E + FACE
                to_x = {-1: slice(0, w * E), 0: slice(w * E, end), 1: slice(end, end + w * E)}[dx]
                value = jnp.zeros(own[0][ts, xs].shape, F32)
                for j in range(BLK):
                    value = select(slot == j, own[j][ts, xs], value)
                    if dx != 0:
                        face = side[j][row : row + FACE * w].reshape(E, w * E, CH)
                        value = select(slot == first + j, face[ts], value)
                    if dt != 0:
                        face = across[j][row : row + FACE * w].reshape(w, FACE, CH)
                        value = select(far == j, face[:, xs], value)
                    if dt != 0 and dx != 0:
                        face = diag[j][corner : corner + E * w * w].reshape(w, w * E, CH)
                        value = select(far == first + j, face, value)
                tile[b, to_t, to_x] = value


def size(part):
    return part[1] * part[3] * E


def span(part, w, dt=0, dx=0):
    t, nt, x, nx = part
    return (
        slice(w + t + dt, w + t + dt + nt),
        slice(E * (w + x + dx), E * (w + x + dx + nx)),
    )


def cut(tile, w, groups, dt=0, dx=0):
    return [
        tile[(b, *span(part, w, dt, dx))].reshape(size(part), CH)
        for b, parts in groups
        for part in parts
    ]


def columns(tile, w, sign, cols, groups):
    for k, (dt, dx) in enumerate(WINDOWS):
        rows = jnp.concatenate(cut(tile, w, groups, sign * dt, sign * dx), axis=0)
        cols[:, k * CH : (k + 1) * CH] = rows.astype(BF)


def shift(value, step):
    y = lax.broadcasted_iota(jnp.int32, value.shape, 0) % E
    moved = pltpu.roll(value, (-step) % value.shape[0], 0)
    return jnp.where(y == (E - 1 if step > 0 else 0), 0.0, moved)


def lanes(value, dy):
    return value[:, (dy + 1) * CH : (dy + 2) * CH]


def gather_y(parts, sign):
    return lanes(parts, 0) + shift(lanes(parts, 1), sign) + shift(lanes(parts, -1), -sign)


def transposed(cols, wide):
    parts = lax.dot_general(
        cols[...], wide[...], (((1,), (1,)), ((), ())), preferred_element_type=F32
    )
    return gather_y(parts, -1)


def arrange(w_ref, tall, wide):
    for k in range(27):
        w, d = divmod(k, 3)
        if tall is not None:
            tall[w * CH : (w + 1) * CH, d * CH : (d + 1) * CH] = w_ref[k]
        if wide is not None:
            wide[d * CH : (d + 1) * CH, w * CH : (w + 1) * CH] = w_ref[k]


def outer(left, right):
    return lax.dot_general(left, right, (((0,), (0,)), ((), ())), preferred_element_type=F32)


def local_math(xcol, gcol, mask, tall, wide, own):
    product = lambda n: jnp.dot(xcol[...], tall[:, n], preferred_element_type=F32)
    parts = [product(slice(0, 2 * CH)), product(slice(2 * CH, 3 * CH))]
    pre = gather_y(jnp.concatenate(parts, axis=1), 1)
    sig = jax.nn.sigmoid(pre)
    hidden = (pre[:own] * sig[:own] * mask[:own]).astype(BF).astype(F32)
    shifted = jnp.concatenate([shift(hidden, -1), hidden, shift(hidden, 1)], axis=1).astype(BF)
    second = outer(shifted, gcol[:own])
    grad_hidden = transposed(gcol, wide)
    grad_pre = (grad_hidden * sig * (1.0 + pre * (1.0 - sig)) * mask).astype(BF).astype(F32)
    mine = grad_pre[:own]
    shifted = jnp.concatenate([shift(mine, 1), mine, shift(mine, -1)], axis=1).astype(BF)
    first = outer(xcol[:own], shifted)
    return grad_pre, first, second


def inner_kernel(
    xg, mask_ref, w1_in, w2_in, gp_ref, first_ref, second_ref, tall, wide1, wide2,
    xtile, gtile, xcol, gcol, w1, w2, sems,
):
    copies = load(sems, [(w1_in, w1), (w2_in, w2)])
    groups = [(b, INNER) for b in EACH]
    xtile[...] = xg[0].astype(F32)
    gtile[...] = xg[1].astype(F32)
    columns(xtile, 0, 1, xcol, groups)
    columns(gtile, 0, -1, gcol, groups)
    mask = jnp.concatenate(cut(mask_ref, 0, groups), axis=0)
    for copy in copies:
        copy.wait()
    arrange(w1, tall, wide1)
    arrange(w2, None, wide2)
    rows = BLK * size(INNER[0])
    grad_pre, first, second = local_math(xcol, gcol, mask, tall, wide2, rows)
    first_ref[...] = first
    second_ref[...] = second
    gp_ref[...] = grad_pre.reshape(gp_ref.shape)


def outer_kernel(
    core, xg, mask_ref, table_in, tall, wide2, inner, first_in, second_in, h0, h1, h2, h3, h4,
    gp_ref, keep_ref, send_ref, xtile, gtile, mtile, xcol, gcol, table, sems,
):
    copies = load(sems, [(table_in, table)])
    owns = [[xg[i, b].astype(F32) for b in EACH] for i in range(2)]
    owns.append([mask_ref[b] for b in EACH])
    targets = [
        (xtile, 2, 0, 0),
        (gtile, 2, 2 * FACE, 4 * E),
        (mtile, 1, 4 * FACE, 8 * E),
    ]
    even = core[0] == 0
    build(targets, owns, table, copies[0].wait, even, (h0, h1, h2, h3, h4))
    groups = [(b, OWN) for b in EACH] + [(b, RIM) for b in EACH]
    columns(xtile, 2, 1, xcol, groups)
    columns(gtile, 2, -1, gcol, groups)
    mask = jnp.concatenate(cut(mtile, 1, groups), axis=0)
    rows = BLK * sum(size(part) for part in OWN)
    grad_pre, first, second = local_math(xcol, gcol, mask, tall, wide2, rows)
    at = 0
    for b, parts in groups:
        for part in parts:
            rows = grad_pre[at : at + size(part)].reshape(part[1], part[3] * E, CH)
            gp_ref[(b, *span(part, 1))] = rows
            at += size(part)
    for b in EACH:
        gp_ref[(b, *span(INNER[0], 1))] = inner[b]
    for k in range(27):
        w, d = divmod(k, 3)
        ws, ds = slice(w * CH, (w + 1) * CH), slice(d * CH, (d + 1) * CH)
        a = second[ds, ws] + second_in[ds, ws]
        b = first[ws, ds] + first_in[ws, ds]
        keep_ref[k] = jnp.where(even, a, b)
        send_ref[k] = jnp.where(even, b, a).astype(BF)


def grad_kernel(gp, mask_ref, cot, wide, out, dcol):
    columns(gp, 1, -1, dcol, [(b, ALL) for b in EACH])
    total = transposed(dcol, wide) * mask_ref[...].reshape(ROWS, CH)
    total = cot[...].astype(F32).reshape(ROWS, CH) + total
    out[...] = total.astype(BF).reshape(BLK, VOX, CH)


def put_half(core, mine, source, first, second, value, sems):
    even = (core[0] == 0) if mine else (core[0] != 0)
    step = 27 // PIECES

    def each(act):
        for flag, target in ((even, second), (~even, first)):
            for n in [act] if isinstance(act, int) else range(PIECES):
                taps = pl.ds(n * step, step)
                copy = pltpu.make_async_copy(value.at[taps], target.at[taps], sems.at[n])
                pl.when(flag)(copy.start if isinstance(act, int) else copy.wait)

    for n in range(PIECES):
        value[n * step : (n + 1) * step] = source[n * step : (n + 1) * step].astype(F32)
        each(n)
    each("all")


def mine_kernel(core, mine, first, second, value, sems):
    put_half(core, True, mine, first, second, value, sems)


def last_kernel(core, other, first_in, second_in, first, second, value, sems):
    put_half(core, False, other, first, second, value, sems)


def in_place(value):
    return pltpu.with_memory_space_constraint(value, pltpu.HBM)


def pack(f, g, occ, sends, when, half, core):
    shapes = [5 * FACE, 5 * FACE, 5 * FACE + 2 * E, 10 * E, 10 * E]
    return pl.pallas_call(
        pack_kernel,
        out_shape=[
            jax.ShapeDtypeStruct((2, BLK, E, FACE, CH), BF),
            jax.ShapeDtypeStruct((BLK, E, FACE, CH), F32),
            *[jax.ShapeDtypeStruct((BLK, rows, CH), BF) for rows in shapes],
        ],
        in_specs=[SM] * 2 + [HB] * 5,
        out_specs=[VM] * 7,
        scratch_shapes=[
            pltpu.VMEM((BLK, VOX, CH), BF),
            pltpu.VMEM((BLK, VOX, CH), BF),
            pltpu.VMEM((BLK, VOX), I32),
            pltpu.SMEM((2, BLK), I32),
            pltpu.SMEM((1, 2 * BLK), I32),
            DMA((5,)),
        ],
        compiler_params=PARAMS,
        name="pack",
    )(half, core, *map(in_place, (f, g, occ, sends, when)))


def inner_pass(xg, mask, w1, w2):
    rows = BLK * size(INNER[0])
    tall, wide = (9 * CH, 3 * CH), (3 * CH, 9 * CH)
    return pl.pallas_call(
        inner_kernel,
        out_shape=[
            jax.ShapeDtypeStruct((BLK, E - 2, (E - 2) * E, CH), F32),
            jax.ShapeDtypeStruct(tall, F32),
            jax.ShapeDtypeStruct(wide, F32),
            jax.ShapeDtypeStruct(tall, BF),
            jax.ShapeDtypeStruct(wide, BF),
            jax.ShapeDtypeStruct(wide, BF),
        ],
        in_specs=[VM] * 2 + [HB] * 2,
        out_specs=[VM] * 6,
        scratch_shapes=[
            pltpu.VMEM((BLK, E, FACE, CH), F32),
            pltpu.VMEM((BLK, E, FACE, CH), F32),
            pltpu.VMEM((rows, 9 * CH), BF),
            pltpu.VMEM((rows, 9 * CH), BF),
            pltpu.VMEM((27, CH, CH), BF),
            pltpu.VMEM((27, CH, CH), BF),
            DMA((2,)),
        ],
        compiler_params=PARAMS,
        name="inner_pass",
    )(xg, mask, *map(in_place, (w1, w2)))


def outer_pass(core, xg, mask, table, tall, wide2, inner, first, second, halos):
    rows = BLK * sum(size(part) for part in OWN + RIM)
    return pl.pallas_call(
        outer_kernel,
        out_shape=[
            jax.ShapeDtypeStruct((BLK, E + 2, (E + 2) * E, CH), F32),
            jax.ShapeDtypeStruct((27, CH, CH), F32),
            jax.ShapeDtypeStruct((27, CH, CH), BF),
        ],
        in_specs=[SM] + [VM] * 2 + [HB] + [VM] * 10,
        out_specs=[VM] * 3,
        scratch_shapes=[
            pltpu.VMEM((BLK, E + 4, (E + 4) * E, CH), F32),
            pltpu.VMEM((BLK, E + 4, (E + 4) * E, CH), F32),
            pltpu.VMEM((BLK, E + 2, (E + 2) * E, CH), F32),
            pltpu.VMEM((rows, 9 * CH), BF),
            pltpu.VMEM((rows, 9 * CH), BF),
            pltpu.SMEM((BLK, 27), I32),
            DMA((1,)),
        ],
        compiler_params=PARAMS,
        name="outer_pass",
    )(core, xg, mask, in_place(table), tall, wide2, inner, first, second, *halos)


def input_grad(gp, mask, cot, wide):
    return pl.pallas_call(
        grad_kernel,
        out_shape=jax.ShapeDtypeStruct((BLK, VOX, CH), BF),
        in_specs=[VM] * 4,
        out_specs=VM,
        scratch_shapes=[pltpu.VMEM((ROWS, 9 * CH), BF)],
        compiler_params=PARAMS,
        name="input_grad",
    )(gp, mask, cot, wide)


PIECES = 3
HALF_SCRATCH = [pltpu.VMEM((27, CH, CH), F32), DMA((PIECES,))]


def mine_half(core, mine):
    weights = jax.ShapeDtypeStruct((27, CH, CH), F32)
    return pl.pallas_call(
        mine_kernel,
        out_shape=[weights, weights],
        in_specs=[SM, VM],
        out_specs=[HB, HB],
        scratch_shapes=HALF_SCRATCH,
        compiler_params=PARAMS,
        name="mine_half",
    )(core, mine)


def last_half(core, other, first, second):
    weights = jax.ShapeDtypeStruct((27, CH, CH), F32)
    return pl.pallas_call(
        last_kernel,
        out_shape=[weights, weights],
        in_specs=[SM, VM, HB, HB],
        out_specs=[HB, HB],
        scratch_shapes=HALF_SCRATCH,
        input_output_aliases={2: 0, 3: 1},
        compiler_params=PARAMS,
        name="last_half",
    )(core, other, first, second)


def swap(value, axis):
    return lax.ppermute(value, axis, [(0, 1), (1, 0)])


def exchange(messages):
    even_side, odd_side, time, even_diag, odd_diag = messages
    size = math.prod(lax.axis_size(axis) for axis in SPACE)
    both = lambda start: [
        pair for i in range(start, size - 1, 2) for pair in ((i, i + 1), (i + 1, i))
    ]
    cross = lambda pairs: [(2 * i + t, 2 * j + 1 - t) for i, j in pairs for t in (0, 1)]
    return (
        lax.ppermute(even_side, SPACE, both(0)),
        lax.ppermute(odd_side, SPACE, both(1)),
        swap(time, TIME),
        lax.ppermute(even_diag, (*SPACE, TIME), cross(both(0))),
        lax.ppermute(odd_diag, (*SPACE, TIME), cross(both(1))),
    )


def spread(value, axes):
    size = math.prod(lax.axis_size(axis) for axis in axes)
    copies = jnp.broadcast_to(value[None], (size, *value.shape))
    return lax.all_to_all(copies, axes, 0, 0)


def reduce_all(keep, send, scale, early):
    total = (keep + swap(send, "c").astype(F32)).astype(BF)
    total, early = lax.optimization_barrier((total, early))
    plane = math.prod(lax.axis_size(axis) for axis in PLANE)
    rows = 27 * CH // plane
    parts = lax.all_to_all(total.reshape(plane, rows, CH), PLANE, 0, 0)
    total = jnp.sum(parts.astype(F32), axis=0)
    depth = lax.axis_size("z")
    parts = lax.all_to_all(total.reshape(depth, rows // depth, CH), "z", 0, 0)
    total = (jnp.sum(parts, axis=0) * scale).astype(BF)
    total = spread(total, ("z",)).reshape(rows, CH)
    mine = spread(total, PLANE).reshape(27, CH, CH)
    return mine, swap(mine, "c"), early


def body(features, cotangent, w_first, w_second, occupancy, neighbors, send_space, send_time):
    f, g = (a.reshape(BLK, VOX, CH) for a in (features, cotangent))
    half = lax.axis_index(TIME).astype(jnp.int32).reshape(1)
    core = lax.axis_index("c").astype(jnp.int32).reshape(1)
    sends = send_space.reshape(2, BLK)
    table = neighbors.reshape(BLK, 27)
    when = send_time.reshape(1, 2 * BLK)
    xg, mask, *messages = pack(f, g, occupancy.reshape(BLK, VOX), sends, when, half, core)
    halos = exchange(messages)
    inner, first, second, tall, wide1, wide2 = inner_pass(xg, mask, w_first, w_second)
    gp, keep, send = outer_pass(
        core, xg, mask, table, tall, wide2, inner, first, second, halos
    )
    out = input_grad(gp, mask, g, wide1)
    devices = math.prod(lax.axis_size(axis) for axis in (*SPACE, TIME))
    scale = 1.0 / math.sqrt(devices * ROWS)
    mine, other, out = reduce_all(keep, send, scale, out)
    first, second = mine_half(core, mine)
    first, second = last_half(core, other, first, second)
    return out.reshape(features.shape), first, second


def solution(mesh):
    fine = Mesh(
        mesh.devices.reshape(*SPLIT.values(), mesh.shape["tm"]), (*SPACE, TIME)
    )
    split = lambda rank: P(SPACE, TIME, *[None] * (rank - 2))
    return jax.shard_map(
        body,
        mesh=fine,
        in_specs=(
            split(5), split(5), P(), P(), split(4), split(4), split(4), split(3),
        ),
        out_specs=(split(5), P(), P()),
        check_vma=False,
    )
```
